256 devices in a mesh: pix: 16 (over x, z_hi, core), frm: 16 (over z_lo, y).
Axes of the slice: x: 4, y: 4, z: 8 (z_hi: 2, z_lo: 4; z = z_hi * 4 + z_lo), core: 2. Of those that a mesh axis runs over, the one named last changes fastest.
Arguments:
- movie: bfloat16 [8192, 4096], P('pix', 'frm'), may hold values from -6 to 6
- taps: float32 [257], replicated, may hold values from -0.25 to 0.25
- scale: float32 [8192], P('pix'), may hold values from 0.3 to 3
- base: float32 [8192], P('pix'), may hold values from 0.2 to 1.5
- spatial: float32 [8192, 256], P('pix'), may hold values from 0.005 to 2
- temporal: float32 [256, 4096], P(None, 'frm'), may hold values from 0.01 to 1.1
Outputs:
- spatial_out: float32 [8192, 256], P('pix')
- temporal_out: float32 [256, 4096], P(None, 'frm')
The draws below stay inside these ranges and needn't reach their ends.
All inputs are finite; a program needn't handle non-finite values.
Results may differ from the reference program's by a relative error of at most 0.0023.
Values may be sent and summed in bfloat16 or wider, within the bound.
A program may use at most 64 MiB of HBM per device.

```python
import math
import jax
import jax.numpy as jnp
from jax import lax

NUM_COMPONENTS = 256
TAPS = 257
ROUNDS = 2
PIXELS = 8192
FRAME_TOTAL = 4096


def geometric_draw(key, shape, lower, upper):
    return jnp.exp(jax.random.uniform(key, shape, jnp.float32, jnp.log(lower), jnp.log(upper)))


def planted(key):
    offset_seed = jax.random.fold_in(key, 101)
    member_key = jax.random.fold_in(offset_seed, 1)
    amplitude_key = jax.random.fold_in(offset_seed, 2)
    activity_seed = jax.random.fold_in(offset_seed, 3)
    const_key = jax.random.fold_in(offset_seed, 4)
    spike_train_key = jax.random.fold_in(offset_seed, 5)
    height_key = jax.random.fold_in(offset_seed, 6)
    starting_key = jax.random.fold_in(offset_seed, 7)
    chance = min(1.0, 4.0 / NUM_COMPONENTS)
    member = jax.random.uniform(member_key, (PIXELS, NUM_COMPONENTS), jnp.float32) < chance
    amplitude = geometric_draw(amplitude_key, (PIXELS, NUM_COMPONENTS), 0.3, 1.2)
    footprint = jnp.where(member, amplitude, 0.0).astype(jnp.float32)
    mean_activity = geometric_draw(activity_seed, (NUM_COMPONENTS, 1), 0.003, 0.03)
    decay_constant = geometric_draw(const_key, (NUM_COMPONENTS, 1), 5.0, 60.0)
    spike_events = jax.random.uniform(spike_train_key, (NUM_COMPONENTS, FRAME_TOTAL), jnp.float32) < mean_activity
    pulse_sizes = jax.random.uniform(height_key, (NUM_COMPONENTS, FRAME_TOTAL), jnp.float32, 0.5, 1.5)
    spikes = jnp.where(spike_events, pulse_sizes, 0.0).astype(jnp.float32)
    decays = jnp.exp(-1.0 / decay_constant[:, 0])
    starting_level = jax.random.uniform(starting_key, (NUM_COMPONENTS,), jnp.float32, 0.0, 1.0) * mean_activity[:, 0] * decay_constant[:, 0]

    def advance(carried, column):
        updated = decays * carried + column
        return (updated, updated)
    unused, result_pixels = lax.scan(advance, starting_level, spikes.T)
    traces = result_pixels.T
    peaks = jnp.maximum(jnp.max(traces, axis=1, keepdims=True), 0.5)
    return (footprint, traces / peaks)


def draw_movie(key, part):
    footprint, traces = planted(key)
    signal = jnp.dot(footprint, traces, precision=lax.Precision.HIGHEST)
    noise_key = jax.random.fold_in(key, 202)
    noise = 0.3 * jax.random.normal(noise_key, (PIXELS, FRAME_TOTAL), jnp.float32)
    return jnp.clip(signal + noise, -6.0, 6.0).astype(jnp.bfloat16)


def draw_spatial(key, part):
    footprint, traces = planted(key)
    perturb_key = jax.random.fold_in(key, 303)
    floor_key = jax.random.fold_in(key, 304)
    perturb = geometric_draw(perturb_key, (PIXELS, NUM_COMPONENTS), 0.6, 1.4)
    floors = geometric_draw(floor_key, (PIXELS, NUM_COMPONENTS), 0.005, 0.05)
    return (footprint * perturb + floors).astype(jnp.float32)


def draw_temporal(key, part):
    footprint, traces = planted(key)
    perturb_key = jax.random.fold_in(key, 403)
    floor_key = jax.random.fold_in(key, 404)
    perturb = geometric_draw(perturb_key, (NUM_COMPONENTS, FRAME_TOTAL), 0.6, 1.4)
    floors = geometric_draw(floor_key, (NUM_COMPONENTS, FRAME_TOTAL), 0.01, 0.1)
    return (0.7 * traces * perturb + floors).astype(jnp.float32)


def block_scale(own_key, shape, pieces, smallest, largest):
    loudness, own = 1.0, jax.random.fold_in(own_key, 6)
    for axis_at, parts in pieces:
        heights = jnp.exp(jax.random.uniform(jax.random.fold_in(own, axis_at), (parts,), jnp.float32, smallest / len(pieces), largest / len(pieces)))
        loudness = loudness * jnp.repeat(heights, shape[axis_at] // parts).reshape([-1 if axis == axis_at else 1 for axis in range(len(shape))])
    return loudness


def gaussian(rng, shape, scale, most, kind=jnp.bfloat16):
    entries = scale * jax.random.normal(rng, shape, jnp.float32)
    return jnp.clip(entries, min=-most, max=most).astype(kind)


def setup_inputs(seed: int = 0) -> dict:
    key_list = jax.random.split(jax.random.key(seed), 7)
    movie = draw_movie(jax.random.fold_in(key_list[6], 71), 0)
    taps = gaussian(key_list[1], (TAPS,), 0.0625, 0.25, jnp.float32)
    scale = jnp.clip(jnp.exp(math.log(3.0) - 2.3025851 * jax.random.uniform(key_list[2], (PIXELS,), jnp.float32) ** block_scale(key_list[2], (PIXELS,), ((0, 16),), -0.2, 0.2)), 0.3, 3.0)
    base = jnp.clip(0.2 + 1.3 * jax.random.uniform(key_list[3], (PIXELS,), jnp.float32) ** block_scale(key_list[3], (PIXELS,), ((0, 16),), -0.2, 0.2), 0.2, 1.5)
    spatial = draw_spatial(jax.random.fold_in(key_list[6], 71), 0)
    temporal = draw_temporal(jax.random.fold_in(key_list[6], 71), 0)
    return {"movie": movie, "taps": taps, "scale": scale, "base": base, "spatial": spatial, "temporal": temporal}


epsilon = 1e-6


def band_matrix(taps, block_len):
    width = taps.shape[0]
    half_width = (width - 1) // 2
    delta = jnp.where(jnp.arange(width, dtype=jnp.int32) == half_width, 1.0, 0.0).astype(jnp.float32)
    coefs = delta - taps
    period = width + block_len
    padded_row = jnp.concatenate([coefs, jnp.zeros((block_len,), jnp.float32)])
    tiled = jnp.tile(padded_row, block_len)
    skewed = tiled[: block_len * (period - 1)].reshape(block_len, period - 1)
    return skewed.T.astype(jnp.bfloat16)


def detrend(padded, taps, scale, base, frame_count):
    half_width = (taps.shape[0] - 1) // 2
    block_len = min(frame_count, 256)
    band = band_matrix(taps, block_len)
    pixel_count = padded.shape[0]

    def one_block(block_id):
        window = lax.dynamic_slice_in_dim(padded, block_id * block_len, block_len + 2 * half_width, 1)
        mixed = jnp.dot(window, band, preferred_element_type=jnp.float32)
        return jnp.maximum(scale[:, None] * mixed + base[:, None], 0.0).astype(jnp.bfloat16)

    blocks = lax.map(one_block, jnp.arange(frame_count // block_len, dtype=jnp.int32))
    return jnp.transpose(blocks, (1, 0, 2)).reshape(pixel_count, frame_count)


def reference(movie, taps, scale, base, spatial, temporal):
    half_width = (taps.shape[0] - 1) // 2
    frame_count = movie.shape[1]
    padded = jnp.pad(movie, ((0, 0), (half_width, half_width)))
    normalised = detrend(padded, taps, scale, base, frame_count)
    spatial_now = spatial
    temporal_now = temporal
    for round_id in range(ROUNDS):
        temporal_copy = temporal_now.astype(jnp.bfloat16)
        numer = jnp.dot(normalised, temporal_copy.T, preferred_element_type=jnp.float32)
        gram = jnp.dot(temporal_now, temporal_now.T, precision=lax.Precision.HIGHEST)
        spatial_now = spatial_now * numer / (jnp.dot(spatial_now, gram, precision=lax.Precision.HIGHEST) + epsilon)
        spatial_copy = spatial_now.astype(jnp.bfloat16)
        numer_t = lax.dot_general(spatial_copy, normalised, (((0,), (0,)), ((), ())), preferred_element_type=jnp.float32)
        gram_t = lax.dot_general(spatial_now, spatial_now, (((0,), (0,)), ((), ())), precision=lax.Precision.HIGHEST)
        temporal_now = temporal_now * numer_t / (jnp.dot(gram_t, temporal_now, precision=lax.Precision.HIGHEST) + epsilon)
    return spatial_now, temporal_now
```

```python
import functools

import jax
import jax.numpy as jnp
from jax import lax
from jax.experimental import pallas as pl
from jax.experimental.pallas import tpu as pltpu
from jax.sharding import PartitionSpec as P

ROUNDS = 2
MESH = pl.DeviceIdType.MESH
F32 = jnp.float32
BF16 = jnp.bfloat16
epsilon = 1e-06

GROUP = 16
CHIPS = 8
PIX = 512
FRM = 256
COMP = 256
ROWS = COMP // GROUP
HALO = 128
TAPS = 257


def frm_steps():
    return sorted(range(1, GROUP), key=lambda k: -(min(k % 4, 4 - k % 4) + k // 4))


def chip_steps():
    return sorted(range(1, CHIPS), key=lambda k: -((k % 2) * 4 + min(k // 2, 4 - k // 2)))


def dot_nn(a, b):
    return lax.dot_general(a, b, (((1,), (0,)), ((), ())), preferred_element_type=F32)


def dot_nt(a, b):
    return lax.dot_general(a, b, (((1,), (1,)), ((), ())), preferred_element_type=F32)


def rows_of(index, count=ROWS):
    return pl.ds(pl.multiple_of(index * count, count), count)


def wait_bytes(ref, sem):
    pltpu.make_async_copy(ref, ref, sem).wait()


def kernel(
    movie_hbm, taps_hbm, scale_hbm, base_hbm, spatial_hbm, temporal_hbm,
    s_out, t_out,
    padded, taps_v, scale_v, base_v, spatial_v, temporal_v,
    coef, norm_t, s_zero_t, s_own, t_own, t_bf,
    gram_part, numer_part, gram_in, numer_in, s_bf,
    mixed_part, core_in, chip_part, chip_in,
    load_sem, halo_send, halo_recv, send_sem, recv_sem,
):
    p = lax.axis_index("pix")
    f = lax.axis_index("frm")
    q, c = lax.div(p, 2), lax.rem(p, 2)

    barrier = pltpu.get_barrier_semaphore()
    for k in range(1, GROUP):
        pl.semaphore_signal(
            barrier, inc=1, device_id=(lax.rem(p + k, GROUP), f), device_id_type=MESH
        )
        pl.semaphore_signal(
            barrier, inc=1, device_id=(p, lax.rem(f + k, GROUP)), device_id_type=MESH
        )

    loads = [
        pltpu.make_async_copy(src, dst, load_sem.at[i])
        for i, (src, dst) in enumerate(
            (
                (movie_hbm, padded.at[:, pl.ds(HALO, FRM)]),
                (temporal_hbm, temporal_v),
                (spatial_hbm, spatial_v),
                (taps_hbm, taps_v),
                (scale_hbm, scale_v),
                (base_hbm, base_v),
            )
        )
    ]
    for copy in loads:
        copy.start()

    def remote(src, dst, phase, target):
        return pltpu.make_async_remote_copy(
            src_ref=src,
            dst_ref=dst,
            send_sem=send_sem.at[phase],
            recv_sem=recv_sem.at[phase],
            device_id=target,
            device_id_type=MESH,
        )

    def frm_scatter(part, inbox, phase):
        for slot, k in enumerate(frm_steps()):
            other = lax.rem(f + k, GROUP)
            remote(part.at[rows_of(other)], inbox.at[slot], phase, (p, other)).start()

    def summed(own, inbox, count):
        total = own
        for slot in range(count):
            total = total + inbox[slot].astype(F32)
        return total

    pl.semaphore_wait(barrier, 2 * (GROUP - 1))
    loads[0].wait()
    to_right = pltpu.make_async_remote_copy(
        src_ref=padded.at[:, pl.ds(FRM, HALO)],
        dst_ref=padded.at[:, pl.ds(0, HALO)],
        send_sem=halo_send.at[0],
        recv_sem=halo_recv.at[0],
        device_id=(p, lax.rem(f + 1, GROUP)),
        device_id_type=MESH,
    )
    to_left = pltpu.make_async_remote_copy(
        src_ref=padded.at[:, pl.ds(HALO, HALO)],
        dst_ref=padded.at[:, pl.ds(HALO + FRM, HALO)],
        send_sem=halo_send.at[1],
        recv_sem=halo_recv.at[1],
        device_id=(p, lax.rem(f + GROUP - 1, GROUP)),
        device_id_type=MESH,
    )

    @pl.when(f < GROUP - 1)
    def _():
        to_right.start()

    @pl.when(f > 0)
    def _():
        to_left.start()

    loads[1].wait()
    t_zero = temporal_v[...].astype(BF16)
    t_bf[0] = t_zero
    gram_part[0] = dot_nt(t_zero, t_zero).astype(BF16)
    frm_scatter(gram_part.at[0], gram_in.at[0], 0)

    @pl.when(f == 0)
    def _():
        padded[:, pl.ds(0, HALO)] = jnp.zeros((PIX, HALO), BF16)

    @pl.when(f == GROUP - 1)
    def _():
        padded[:, pl.ds(HALO + FRM, HALO)] = jnp.zeros((PIX, HALO), BF16)

    for copy in loads[2:]:
        copy.wait()
    coef[...] = jnp.zeros_like(coef)
    centre = lax.broadcasted_iota(jnp.int32, (1, TAPS), 1) == HALO
    coef[:, pl.ds(0, TAPS)] = jnp.where(centre, 1.0, 0.0).astype(F32) - taps_v[...]
    band_t = pltpu.roll(
        jnp.broadcast_to(coef[...], (FRM, 2 * FRM)), 0, 1, stride=1, stride_axis=0
    ).astype(BF16)
    spatial_t = spatial_v[...].T
    s_zero_t[...] = spatial_t
    s_bf[0] = spatial_t.astype(BF16)
    s_own[...] = s_zero_t[rows_of(f), :]
    comp_block = c * CHIPS + q
    t_own[...] = temporal_v[rows_of(comp_block), :]

    @pl.when(f > 0)
    def _():
        to_right.wait_recv()

    @pl.when(f < GROUP - 1)
    def _():
        to_left.wait_recv()

    mixed = dot_nt(band_t, padded[...])
    norm_t[...] = jnp.maximum(scale_v[...] * mixed + base_v[...], 0.0).astype(BF16)

    for r in range(ROUNDS):
        base_phase = 1 + 6 * r
        numer_part[r] = dot_nn(t_bf[r], norm_t[...]).astype(BF16)
        frm_scatter(numer_part.at[r], numer_in.at[r], base_phase)
        if r:
            gram_part[r] = dot_nt(t_bf[r], t_bf[r]).astype(BF16)
            frm_scatter(gram_part.at[r], gram_in.at[r], base_phase + 1)
        gram_phase = base_phase + 1 if r else 0
        wait_bytes(gram_in.at[r], recv_sem.at[gram_phase])
        gram = summed(gram_part[r, rows_of(f), :].astype(F32), gram_in.at[r], GROUP - 1)
        denom = dot_nn(gram.astype(BF16), s_bf[r]) + epsilon
        wait_bytes(numer_in.at[r], recv_sem.at[base_phase])
        numer = summed(numer_part[r, rows_of(f), :].astype(F32), numer_in.at[r], GROUP - 1)
        s_new = s_own[...] * numer / denom
        s_own[...] = s_new
        s_bf[r + 1, rows_of(f), :] = s_new.astype(BF16)
        mine = s_bf.at[r + 1, rows_of(f)]
        for k in frm_steps():
            remote(mine, mine, base_phase + 2, (p, lax.rem(f + k, GROUP))).start()
        wait_bytes(s_bf.at[r + 1, pl.ds(0, COMP - ROWS)], recv_sem.at[base_phase + 2])

        s_now = s_bf[r + 1]
        mixed_part[r, :, pl.ds(0, FRM)] = dot_nt(s_now, norm_t[...]).astype(BF16)
        mixed_part[r, :, pl.ds(FRM, COMP)] = dot_nt(s_now, s_now).astype(BF16)
        half = COMP // 2
        remote(
            mixed_part.at[r, rows_of(1 - c, half)],
            core_in.at[r],
            base_phase + 3,
            (2 * q + 1 - c, f),
        ).start()
        if r == ROUNDS - 1:
            s_out[...] = s_now.astype(F32).T.astype(BF16)
        wait_bytes(core_in.at[r], recv_sem.at[base_phase + 3])
        chip_sum = mixed_part[r, rows_of(c, half), :].astype(F32) + core_in[r].astype(F32)
        chip_part[r] = chip_sum.astype(BF16)
        for slot, k in enumerate(chip_steps()):
            kx, kz = k // 2, k % 2
            x, zh = lax.div(q, 2), lax.rem(q, 2)
            other = lax.rem(x + kx, 4) * 2 + lax.rem(zh + kz, 2)
            remote(
                chip_part.at[r, rows_of(other)],
                chip_in.at[r, slot],
                base_phase + 4,
                (2 * other + c, f),
            ).start()
        wait_bytes(chip_in.at[r], recv_sem.at[base_phase + 4])
        total = summed(chip_part[r, rows_of(q), :].astype(F32), chip_in.at[r], CHIPS - 1)
        denom_t = dot_nn(total[:, FRM:].astype(BF16), t_bf[r]) + epsilon
        t_new = t_own[...] * total[:, :FRM] / denom_t
        t_own[...] = t_new
        t_bf[r + 1, rows_of(comp_block), :] = t_new.astype(BF16)
        own_rows = t_bf.at[r + 1, rows_of(comp_block)]
        for k in sorted(range(1, GROUP), key=lambda k: -(k % 4 // 2)):
            remote(own_rows, own_rows, base_phase + 5, (lax.rem(p + k, GROUP), f)).start()
        wait_bytes(t_bf.at[r + 1, pl.ds(0, COMP - ROWS)], recv_sem.at[base_phase + 5])

    t_out[...] = t_bf[ROUNDS]

    @pl.when(f < GROUP - 1)
    def _():
        to_right.wait_send()

    @pl.when(f > 0)
    def _():
        to_left.wait_send()

    wait_bytes(gram_in.at[0], send_sem.at[0])
    for r in range(ROUNDS):
        base_phase = 1 + 6 * r
        wait_bytes(numer_in.at[r], send_sem.at[base_phase])
        if r:
            wait_bytes(gram_in.at[r], send_sem.at[base_phase + 1])
        wait_bytes(s_bf.at[r + 1, pl.ds(0, COMP - ROWS)], send_sem.at[base_phase + 2])
        wait_bytes(core_in.at[r], send_sem.at[base_phase + 3])
        wait_bytes(chip_in.at[r], send_sem.at[base_phase + 4])
        wait_bytes(t_bf.at[r + 1, pl.ds(0, COMP - ROWS)], send_sem.at[base_phase + 5])


def on_device(movie, taps, scale, base, spatial, temporal):
    phases = 1 + 6 * ROUNDS
    s, t = pl.pallas_call(
        kernel,
        out_shape=(
            jax.ShapeDtypeStruct((PIX, COMP), BF16),
            jax.ShapeDtypeStruct((COMP, FRM), BF16),
        ),
        in_specs=[pl.BlockSpec(memory_space=pl.ANY)] * 6,
        out_specs=(pl.BlockSpec(memory_space=pltpu.VMEM),) * 2,
        scratch_shapes=[
            pltpu.VMEM((PIX, 2 * FRM), BF16),
            pltpu.VMEM((1, TAPS), F32),
            pltpu.VMEM((1, PIX), F32),
            pltpu.VMEM((1, PIX), F32),
            pltpu.VMEM((PIX, COMP), F32),
            pltpu.VMEM((COMP, FRM), F32),
            pltpu.VMEM((1, 2 * FRM), F32),
            pltpu.VMEM((FRM, PIX), BF16),
            pltpu.VMEM((COMP, PIX), F32),
            pltpu.VMEM((ROWS, PIX), F32),
            pltpu.VMEM((ROWS, FRM), F32),
            pltpu.VMEM((ROUNDS + 1, COMP, FRM), BF16),
            pltpu.VMEM((ROUNDS, COMP, COMP), BF16),
            pltpu.VMEM((ROUNDS, COMP, PIX), BF16),
            pltpu.VMEM((ROUNDS, GROUP - 1, ROWS, COMP), BF16),
            pltpu.VMEM((ROUNDS, GROUP - 1, ROWS, PIX), BF16),
            pltpu.VMEM((ROUNDS + 1, COMP, PIX), BF16),
            pltpu.VMEM((ROUNDS, COMP, FRM + COMP), BF16),
            pltpu.VMEM((ROUNDS, COMP // 2, FRM + COMP), BF16),
            pltpu.VMEM((ROUNDS, COMP // 2, FRM + COMP), BF16),
            pltpu.VMEM((ROUNDS, CHIPS - 1, ROWS, FRM + COMP), BF16),
            pltpu.SemaphoreType.DMA((6,)),
            pltpu.SemaphoreType.DMA((2,)),
            pltpu.SemaphoreType.DMA((2,)),
            pltpu.SemaphoreType.DMA((phases,)),
            pltpu.SemaphoreType.DMA((phases,)),
        ],
        compiler_params=pltpu.CompilerParams(
            collective_id=0, has_side_effects=True, vmem_limit_bytes=32 << 20
        ),
    )(movie, taps[None], scale[None], base[None], spatial, temporal)
    return s.astype(F32), t.astype(F32)


def solution(mesh):
    placed = (P("pix", "frm"), P(), P("pix"), P("pix"), P("pix", None), P(None, "frm"))
    return jax.shard_map(
        on_device,
        mesh=mesh,
        in_specs=placed,
        out_specs=(P("pix", None), P(None, "frm")),
        check_vma=False,
    )
```

```python
import functools

import jax
import jax.numpy as jnp
from jax import lax
from jax.experimental import pallas as pl
from jax.experimental.pallas import tpu as pltpu
from jax.sharding import PartitionSpec as P

ROUNDS = 2
MESH = pl.DeviceIdType.MESH
F32 = jnp.float32
BF16 = jnp.bfloat16
epsilon = 1e-06

GROUP = 16
CHIPS = 8
PIX = 512
FRM = 256
COMP = 256
ROWS = COMP // GROUP
HALO = 128
TAPS = 257


def frm_steps():
    return sorted(range(1, GROUP), key=lambda k: -(min(k % 4, 4 - k % 4) + k // 4))


def chip_steps():
    return sorted(range(1, CHIPS), key=lambda k: -((k % 2) * 4 + min(k // 2, 4 - k // 2)))


def dot_nn(a, b):
    return lax.dot_general(a, b, (((1,), (0,)), ((), ())), preferred_element_type=F32)


def dot_nt(a, b):
    return lax.dot_general(a, b, (((1,), (1,)), ((), ())), preferred_element_type=F32)


def product(gram, whole, block, own, own_copy):
    high = gram.astype(BF16)
    low = (gram - high.astype(F32)).astype(BF16)
    both = dot_nn(jnp.concatenate([high, low], axis=0), whole)
    row = lax.broadcasted_iota(jnp.int32, gram.shape, 0)
    column = lax.broadcasted_iota(jnp.int32, gram.shape, 1)
    diagonal = jnp.sum(jnp.where(column == row + block * ROWS, gram, 0.0), axis=1, keepdims=True)
    return both[:ROWS] + both[ROWS:] + diagonal * (own - own_copy.astype(F32))


def rows_of(index, count=ROWS):
    return pl.ds(pl.multiple_of(index * count, count), count)


def wait_bytes(ref, sem):
    pltpu.make_async_copy(ref, ref, sem).wait()


def kernel(
    movie_hbm, taps_hbm, scale_hbm, base_hbm, spatial_hbm, temporal_hbm,
    s_out, t_out,
    padded, taps_v, scale_v, base_v, spatial_v, temporal_v,
    coef, norm_t, s_zero_t, s_own, t_own, t_bf,
    gram_part, numer_part, gram_in, numer_in, s_bf,
    mixed_part, core_in, chip_part, chip_in,
    load_sem, halo_send, halo_recv, send_sem, recv_sem,
):
    p = lax.axis_index("pix")
    f = lax.axis_index("frm")
    q, c = lax.div(p, 2), lax.rem(p, 2)

    barrier = pltpu.get_barrier_semaphore()
    for k in range(1, GROUP):
        pl.semaphore_signal(
            barrier, inc=1, device_id=(lax.rem(p + k, GROUP), f), device_id_type=MESH
        )
        pl.semaphore_signal(
            barrier, inc=1, device_id=(p, lax.rem(f + k, GROUP)), device_id_type=MESH
        )

    loads = [
        pltpu.make_async_copy(src, dst, load_sem.at[i])
        for i, (src, dst) in enumerate(
            (
                (movie_hbm, padded.at[:, pl.ds(HALO, FRM)]),
                (temporal_hbm, temporal_v),
                (spatial_hbm, spatial_v),
                (taps_hbm, taps_v),
                (scale_hbm, scale_v),
                (base_hbm, base_v),
            )
        )
    ]
    for copy in loads:
        copy.start()

    def remote(src, dst, phase, target):
        return pltpu.make_async_remote_copy(
            src_ref=src,
            dst_ref=dst,
            send_sem=send_sem.at[phase],
            recv_sem=recv_sem.at[phase],
            device_id=target,
            device_id_type=MESH,
        )

    def frm_scatter(part, inbox, phase):
        for slot, k in enumerate(frm_steps()):
            other = lax.rem(f + k, GROUP)
            remote(part.at[rows_of(other)], inbox.at[slot], phase, (p, other)).start()

    def summed(own, inbox, count):
        total = own
        for slot in range(count):
            total = total + inbox[slot].astype(F32)
        return total

    pl.semaphore_wait(barrier, 2 * (GROUP - 1))
    loads[0].wait()
    to_right = pltpu.make_async_remote_copy(
        src_ref=padded.at[:, pl.ds(FRM, HALO)],
        dst_ref=padded.at[:, pl.ds(0, HALO)],
        send_sem=halo_send.at[0],
        recv_sem=halo_recv.at[0],
        device_id=(p, lax.rem(f + 1, GROUP)),
        device_id_type=MESH,
    )
    to_left = pltpu.make_async_remote_copy(
        src_ref=padded.at[:, pl.ds(HALO, HALO)],
        dst_ref=padded.at[:, pl.ds(HALO + FRM, HALO)],
        send_sem=halo_send.at[1],
        recv_sem=halo_recv.at[1],
        device_id=(p, lax.rem(f + GROUP - 1, GROUP)),
        device_id_type=MESH,
    )

    @pl.when(f < GROUP - 1)
    def _():
        to_right.start()

    @pl.when(f > 0)
    def _():
        to_left.start()

    loads[1].wait()
    t_zero = temporal_v[...].astype(BF16)
    t_bf[0] = t_zero
    gram_part[0] = dot_nt(t_zero, t_zero).astype(BF16)
    frm_scatter(gram_part.at[0], gram_in.at[0], 0)

    @pl.when(f == 0)
    def _():
        padded[:, pl.ds(0, HALO)] = jnp.zeros((PIX, HALO), BF16)

    @pl.when(f == GROUP - 1)
    def _():
        padded[:, pl.ds(HALO + FRM, HALO)] = jnp.zeros((PIX, HALO), BF16)

    for copy in loads[2:]:
        copy.wait()
    coef[...] = jnp.zeros_like(coef)
    centre = lax.broadcasted_iota(jnp.int32, (1, TAPS), 1) == HALO
    coef[:, pl.ds(0, TAPS)] = jnp.where(centre, 1.0, 0.0).astype(F32) - taps_v[...][None]
    band_t = pltpu.roll(
        jnp.broadcast_to(coef[...], (FRM, 2 * FRM)), 0, 1, stride=1, stride_axis=0
    ).astype(BF16)
    spatial_t = spatial_v[...].T
    s_zero_t[...] = spatial_t
    s_bf[0] = spatial_t.astype(BF16)
    s_own[...] = s_zero_t[rows_of(f), :]
    comp_block = c * CHIPS + q
    t_own[...] = temporal_v[rows_of(comp_block), :]

    @pl.when(f > 0)
    def _():
        to_right.wait_recv()

    @pl.when(f < GROUP - 1)
    def _():
        to_left.wait_recv()

    mixed = dot_nt(band_t, padded[...])
    norm_t[...] = jnp.maximum(scale_v[...][None] * mixed + base_v[...][None], 0.0).astype(BF16)

    for r in range(ROUNDS):
        base_phase = 1 + 6 * r
        numer_part[r] = dot_nn(t_bf[r], norm_t[...]).astype(BF16)
        frm_scatter(numer_part.at[r], numer_in.at[r], base_phase)
        if r:
            gram_part[r] = dot_nt(t_bf[r], t_bf[r]).astype(BF16)
            frm_scatter(gram_part.at[r], gram_in.at[r], base_phase + 1)
        gram_phase = base_phase + 1 if r else 0
        wait_bytes(gram_in.at[r], recv_sem.at[gram_phase])
        gram = summed(gram_part[r, rows_of(f), :].astype(F32), gram_in.at[r], GROUP - 1)
        denom = product(gram, s_bf[r], f, s_own[...], s_bf[r, rows_of(f), :]) + epsilon
        wait_bytes(numer_in.at[r], recv_sem.at[base_phase])
        numer = summed(numer_part[r, rows_of(f), :].astype(F32), numer_in.at[r], GROUP - 1)
        s_new = s_own[...] * numer / denom
        s_own[...] = s_new
        s_bf[r + 1, rows_of(f), :] = s_new.astype(BF16)
        mine = s_bf.at[r + 1, rows_of(f)]
        for k in frm_steps():
            remote(mine, mine, base_phase + 2, (p, lax.rem(f + k, GROUP))).start()
        wait_bytes(s_bf.at[r + 1, pl.ds(0, COMP - ROWS)], recv_sem.at[base_phase + 2])

        s_now = s_bf[r + 1]
        mixed_part[r, :, pl.ds(0, FRM)] = dot_nt(s_now, norm_t[...]).astype(BF16)
        mixed_part[r, :, pl.ds(FRM, COMP)] = dot_nt(s_now, s_now).astype(BF16)
        half = COMP // 2
        remote(
            mixed_part.at[r, rows_of(1 - c, half)],
            core_in.at[r],
            base_phase + 3,
            (2 * q + 1 - c, f),
        ).start()
        if r == ROUNDS - 1:
            s_out[...] = s_now.astype(F32).T.astype(BF16)
        wait_bytes(core_in.at[r], recv_sem.at[base_phase + 3])
        chip_sum = mixed_part[r, rows_of(c, half), :].astype(F32) + core_in[r].astype(F32)
        chip_part[r] = chip_sum.astype(BF16)
        for slot, k in enumerate(chip_steps()):
            kx, kz = k // 2, k % 2
            x, zh = lax.div(q, 2), lax.rem(q, 2)
            other = lax.rem(x + kx, 4) * 2 + lax.rem(zh + kz, 2)
            remote(
                chip_part.at[r, rows_of(other)],
                chip_in.at[r, slot],
                base_phase + 4,
                (2 * other + c, f),
            ).start()
        wait_bytes(chip_in.at[r], recv_sem.at[base_phase + 4])
        total = summed(chip_part[r, rows_of(q), :].astype(F32), chip_in.at[r], CHIPS - 1)
        gram_t = total[:, FRM:]
        t_copy = t_bf[r, rows_of(comp_block), :]
        denom_t = product(gram_t, t_bf[r], comp_block, t_own[...], t_copy) + epsilon
        t_new = t_own[...] * total[:, :FRM] / denom_t
        t_own[...] = t_new
        t_bf[r + 1, rows_of(comp_block), :] = t_new.astype(BF16)
        own_rows = t_bf.at[r + 1, rows_of(comp_block)]
        for k in sorted(range(1, GROUP), key=lambda k: -(k % 4 // 2)):
            remote(own_rows, own_rows, base_phase + 5, (lax.rem(p + k, GROUP), f)).start()
        wait_bytes(t_bf.at[r + 1, pl.ds(0, COMP - ROWS)], recv_sem.at[base_phase + 5])

    t_out[...] = t_bf[ROUNDS]

    @pl.when(f < GROUP - 1)
    def _():
        to_right.wait_send()

    @pl.when(f > 0)
    def _():
        to_left.wait_send()

    wait_bytes(gram_in.at[0], send_sem.at[0])
    for r in range(ROUNDS):
        base_phase = 1 + 6 * r
        wait_bytes(numer_in.at[r], send_sem.at[base_phase])
        if r:
            wait_bytes(gram_in.at[r], send_sem.at[base_phase + 1])
        wait_bytes(s_bf.at[r + 1, pl.ds(0, COMP - ROWS)], send_sem.at[base_phase + 2])
        wait_bytes(core_in.at[r], send_sem.at[base_phase + 3])
        wait_bytes(chip_in.at[r], send_sem.at[base_phase + 4])
        wait_bytes(t_bf.at[r + 1, pl.ds(0, COMP - ROWS)], send_sem.at[base_phase + 5])


def widen(s_hbm, t_hbm, s_out, t_out, s_v, t_v, s_w, t_w, sem):
    into = [
        pltpu.make_async_copy(t_hbm, t_v, sem.at[0]),
        pltpu.make_async_copy(s_hbm, s_v, sem.at[1]),
    ]
    out = [
        pltpu.make_async_copy(t_w, t_out, sem.at[2]),
        pltpu.make_async_copy(s_w, s_out, sem.at[3]),
    ]
    for copy in into:
        copy.start()
    for narrow, wide, copy, back in zip((t_v, s_v), (t_w, s_w), into, out):
        copy.wait()
        wide[...] = narrow[...].astype(F32)
        back.start()
    for back in out:
        back.wait()


def on_device(movie, taps, scale, base, spatial, temporal):
    phases = 1 + 6 * ROUNDS
    s, t = pl.pallas_call(
        kernel,
        out_shape=(
            jax.ShapeDtypeStruct((PIX, COMP), BF16),
            jax.ShapeDtypeStruct((COMP, FRM), BF16),
        ),
        in_specs=[pl.BlockSpec(memory_space=pltpu.HBM)] * 6,
        out_specs=(pl.BlockSpec(memory_space=pltpu.VMEM),) * 2,
        scratch_shapes=[
            pltpu.VMEM((PIX, 2 * FRM), BF16),
            pltpu.VMEM((TAPS,), F32),
            pltpu.VMEM((PIX,), F32),
            pltpu.VMEM((PIX,), F32),
            pltpu.VMEM((PIX, COMP), F32),
            pltpu.VMEM((COMP, FRM), F32),
            pltpu.VMEM((1, 2 * FRM), F32),
            pltpu.VMEM((FRM, PIX), BF16),
            pltpu.VMEM((COMP, PIX), F32),
            pltpu.VMEM((ROWS, PIX), F32),
            pltpu.VMEM((ROWS, FRM), F32),
            pltpu.VMEM((ROUNDS + 1, COMP, FRM), BF16),
            pltpu.VMEM((ROUNDS, COMP, COMP), BF16),
            pltpu.VMEM((ROUNDS, COMP, PIX), BF16),
            pltpu.VMEM((ROUNDS, GROUP - 1, ROWS, COMP), BF16),
            pltpu.VMEM((ROUNDS, GROUP - 1, ROWS, PIX), BF16),
            pltpu.VMEM((ROUNDS + 1, COMP, PIX), BF16),
            pltpu.VMEM((ROUNDS, COMP, FRM + COMP), BF16),
            pltpu.VMEM((ROUNDS, COMP // 2, FRM + COMP), BF16),
            pltpu.VMEM((ROUNDS, COMP // 2, FRM + COMP), BF16),
            pltpu.VMEM((ROUNDS, CHIPS - 1, ROWS, FRM + COMP), BF16),
            pltpu.SemaphoreType.DMA((6,)),
            pltpu.SemaphoreType.DMA((2,)),
            pltpu.SemaphoreType.DMA((2,)),
            pltpu.SemaphoreType.DMA((phases,)),
            pltpu.SemaphoreType.DMA((phases,)),
        ],
        compiler_params=pltpu.CompilerParams(
            collective_id=0, has_side_effects=True, vmem_limit_bytes=60 << 20
        ),
    )(movie, taps, scale, base, spatial, temporal)
    return pl.pallas_call(
        widen,
        out_shape=(
            jax.ShapeDtypeStruct((PIX, COMP), F32),
            jax.ShapeDtypeStruct((COMP, FRM), F32),
        ),
        in_specs=[pl.BlockSpec(memory_space=pltpu.HBM)] * 2,
        out_specs=(pl.BlockSpec(memory_space=pltpu.HBM),) * 2,
        scratch_shapes=[
            pltpu.VMEM((PIX, COMP), BF16),
            pltpu.VMEM((COMP, FRM), BF16),
            pltpu.VMEM((PIX, COMP), F32),
            pltpu.VMEM((COMP, FRM), F32),
            pltpu.SemaphoreType.DMA((4,)),
        ],
        compiler_params=pltpu.CompilerParams(vmem_limit_bytes=60 << 20),
    )(s, t)


def solution(mesh):
    placed = (P("pix", "frm"), P(), P("pix"), P("pix"), P("pix", None), P(None, "frm"))
    return jax.shard_map(
        on_device,
        mesh=mesh,
        in_specs=placed,
        out_specs=(P("pix", None), P(None, "frm")),
        check_vma=False,
    )
```

```python
import functools

import jax
import jax.numpy as jnp
from jax import lax
from jax.experimental import pallas as pl
from jax.experimental.pallas import tpu as pltpu
from jax.sharding import PartitionSpec as P

ROUNDS = 2
MESH = pl.DeviceIdType.MESH
F32 = jnp.float32
BF16 = jnp.bfloat16
epsilon = 1e-06

GROUP = 16
CHIPS = 8
PIX = 512
FRM = 256
COMP = 256
ROWS = COMP // GROUP
HALO = 128
SPLIT = 2
PART = PIX // SPLIT
HALF = COMP // 2
TAPS = 257


def far_first(steps, hops):
    return sorted(steps, key=lambda step: -hops(*step))


FRM_STEPS = far_first(
    [(dzl, dy) for dzl in range(4) for dy in range(4) if dzl or dy],
    lambda dzl, dy: dzl + min(dy, 4 - dy),
)
CHIP_STEPS = far_first(
    [(dx, dzh) for dx in range(4) for dzh in range(2) if dx or dzh],
    lambda dx, dzh: min(dx, 4 - dx) + 4 * dzh,
)
PIX_STEPS = far_first(
    [(dx, dzh, dc) for dx in range(4) for dzh in range(2) for dc in range(2) if dx or dzh or dc],
    lambda dx, dzh, dc: min(dx, 4 - dx) + 4 * dzh + 0.5 * dc,
)


def dot_nn(a, b):
    return lax.dot_general(a, b, (((1,), (0,)), ((), ())), preferred_element_type=F32)


def dot_nt(a, b):
    return lax.dot_general(a, b, (((1,), (1,)), ((), ())), preferred_element_type=F32)


def split(value):
    high = value.astype(BF16)
    return high, (value - high.astype(F32)).astype(BF16)


def product(gram, wholes, block, owns, own_copies):
    terms = jnp.concatenate(split(gram), axis=0)
    row = lax.broadcasted_iota(jnp.int32, gram.shape, 0)
    column = lax.broadcasted_iota(jnp.int32, gram.shape, 1)
    diagonal = jnp.sum(jnp.where(column == row + block * ROWS, gram, 0.0), axis=1, keepdims=True)
    results = []
    for whole, own, copy in zip(wholes, owns, own_copies):
        both = dot_nn(terms, whole)
        results.append(both[:ROWS] + both[ROWS:] + diagonal * (own - copy.astype(F32)))
    return results


def rows_of(index, count=ROWS):
    return pl.ds(pl.multiple_of(index * count, count), count)


def wait_bytes(ref, sem):
    pltpu.make_async_copy(ref, ref, sem).wait()


def summed(inbox, count):
    total = inbox[0].astype(F32)
    for slot in range(1, count):
        total = total + inbox[slot].astype(F32)
    return total


NUMER, GRAM, SHARE, LOW, CORE_GRAM, CORE, CHIP, NEAR, FAR, RELAY = 0, 2, 3, 5, 7, 8, 9, 10, 11, 12
PHASES = 14


def kernel(
    movie_hbm, taps_hbm, scale_hbm, base_hbm, spatial_hbm, temporal_hbm,
    s_out, t_out,
    padded, taps_v, scale_v, base_v, spatial_v, temporal_v,
    coef, norm_t, s_zero_t, s_own, t_own, t_bf,
    gram_part, gram_in, gram_own, numer_part, numer_in, s_bf, s_low,
    mixed_part, core_in, chip_part, chip_in, s_wide, t_wide,
    load_sem, halo_send, halo_recv, send_sem, recv_sem, out_sem,
):
    p = lax.axis_index("pix")
    f = lax.axis_index("frm")
    x, zh, c = lax.div(p, 4), lax.rem(lax.div(p, 2), 2), lax.rem(p, 2)
    zl, y = lax.div(f, 4), lax.rem(f, 4)
    pix_block = zh * 4 + x
    t_block = c * CHIPS + pix_block

    def pix_at(dx, dzh, dc):
        return lax.rem(x + dx, 4), lax.rem(zh + dzh, 2), lax.rem(c + dc, 2)

    def pix_device(ox, ozh, oc):
        return ((ox * 2 + ozh) * 2 + oc, f)

    def frm_at(dzl, dy):
        return lax.rem(zl + dzl, 4) * 4 + lax.rem(y + dy, 4)

    barrier = pltpu.get_barrier_semaphore()
    for k in range(1, GROUP):
        pl.semaphore_signal(
            barrier, inc=1, device_id=(lax.rem(p + k, GROUP), f), device_id_type=MESH
        )
        pl.semaphore_signal(
            barrier, inc=1, device_id=(p, lax.rem(f + k, GROUP)), device_id_type=MESH
        )

    loads = [
        pltpu.make_async_copy(src, dst, load_sem.at[i])
        for i, (src, dst) in enumerate(
            (
                (movie_hbm, padded.at[:, pl.ds(HALO, FRM)]),
                (temporal_hbm, temporal_v),
                (spatial_hbm, spatial_v),
                (taps_hbm, taps_v),
                (scale_hbm, scale_v),
                (base_hbm, base_v),
            )
        )
    ]
    for copy in loads:
        copy.start()

    def remote(src, dst, sem, target):
        return pltpu.make_async_remote_copy(
            src_ref=src,
            dst_ref=dst,
            send_sem=send_sem.at[sem],
            recv_sem=recv_sem.at[sem],
            device_id=target,
            device_id_type=MESH,
        )

    pl.semaphore_wait(barrier, 2 * (GROUP - 1))
    loads[0].wait()
    halos = []
    for h in range(SPLIT):
        pixels = pl.ds(h * PART, PART)
        for side, (source, target, step) in enumerate(
            ((FRM, 0, 1), (HALO, HALO + FRM, GROUP - 1))
        ):
            halos.append(
                pltpu.make_async_remote_copy(
                    src_ref=padded.at[pixels, pl.ds(source, HALO)],
                    dst_ref=padded.at[pixels, pl.ds(target, HALO)],
                    send_sem=halo_send.at[2 * h + side],
                    recv_sem=halo_recv.at[2 * h + side],
                    device_id=(p, lax.rem(f + step, GROUP)),
                    device_id_type=MESH,
                )
            )
    has_right, has_left = f < GROUP - 1, f > 0

    @pl.when(has_right)
    def _():
        for copy in halos[0::2]:
            copy.start()

    @pl.when(has_left)
    def _():
        for copy in halos[1::2]:
            copy.start()

    def send_gram(r):
        t_now = t_bf[r]
        t_half = t_bf[r, rows_of(c, HALF), :]
        gram_part[r] = dot_nt(t_now, t_half).astype(BF16)
        for dzl, dy in FRM_STEPS:
            other = frm_at(dzl, dy)
            remote(
                gram_part.at[r, rows_of(other)], gram_in.at[r, f], r * PHASES + GRAM, (p, other)
            ).start()
        gram_in[r, f] = gram_part[r, rows_of(f), :]

    def finish_gram(r):
        wait_bytes(gram_in.at[r, pl.ds(0, GROUP - 1)], recv_sem.at[r * PHASES + GRAM])
        half = pl.ds(pl.multiple_of(c * HALF, HALF), HALF)
        gram_own[r, :, half] = summed(gram_in.at[r], GROUP)
        mine = gram_own.at[r, :, half]
        copy = remote(mine, mine, r * PHASES + CORE_GRAM, pix_device(x, zh, 1 - c))
        copy.start()
        copy.wait_recv()

    loads[1].wait()
    t_bf[0] = temporal_v[...].astype(BF16)
    send_gram(0)

    @pl.when(f == 0)
    def _():
        padded[:, pl.ds(0, HALO)] = jnp.zeros((PIX, HALO), BF16)

    @pl.when(f == GROUP - 1)
    def _():
        padded[:, pl.ds(HALO + FRM, HALO)] = jnp.zeros((PIX, HALO), BF16)

    for copy in loads[2:]:
        copy.wait()
    coef[...] = jnp.zeros_like(coef)
    centre = lax.broadcasted_iota(jnp.int32, (1, TAPS), 1) == HALO
    coef[:, pl.ds(0, TAPS)] = jnp.where(centre, 1.0, 0.0).astype(F32) - taps_v[...][None]
    band_t = pltpu.roll(
        jnp.broadcast_to(coef[...], (FRM, 2 * FRM)), 0, 1, stride=1, stride_axis=0
    ).astype(BF16)
    spatial_t = spatial_v[...].T
    for h in range(SPLIT):
        s_zero_t[h] = spatial_t[:, h * PART : (h + 1) * PART]
        s_bf[0, h] = s_zero_t[h].astype(BF16)
        s_own[h] = s_zero_t[h, rows_of(f), :]
    t_own[...] = temporal_v[rows_of(t_block), :]

    def send_numer(r, h, others):
        for other in others:
            remote(
                numer_part.at[r, h, rows_of(other)],
                numer_in.at[r, h, f],
                r * PHASES + NUMER + h,
                (p, other),
            ).start()

    for h in range(SPLIT):
        pixels = pl.ds(h * PART, PART)

        @pl.when(has_left)
        def _():
            halos[2 * h].wait_recv()

        @pl.when(has_right)
        def _():
            halos[2 * h + 1].wait_recv()

        mixed = dot_nt(band_t, padded[pixels, :])
        scaled = scale_v[pixels][None] * mixed + base_v[pixels][None]
        norm_t[h] = jnp.maximum(scaled, 0.0).astype(BF16)
        numer_part[0, h] = dot_nn(t_bf[0], norm_t[h]).astype(BF16)
        send_numer(0, h, [frm_at(dzl, dy) for dzl, dy in FRM_STEPS])
        numer_in[0, h, f] = numer_part[0, h, rows_of(f), :]

    for r in range(ROUNDS):
        last = r == ROUNDS - 1
        at = r * PHASES
        finish_gram(r)
        denoms = product(
            gram_own[r],
            [s_bf[r, h] for h in range(SPLIT)],
            f,
            [s_own[h] for h in range(SPLIT)],
            [s_bf[r, h, rows_of(f), :] for h in range(SPLIT)],
        )
        for h in range(SPLIT):
            wait_bytes(numer_in.at[r, h, pl.ds(0, GROUP - 1)], recv_sem.at[at + NUMER + h])
            numer = summed(numer_in.at[r, h], GROUP)
            s_new = s_own[h] * numer / (denoms[h] + epsilon)
            s_own[h] = s_new
            high, low = split(s_new)
            s_bf[r + 1, h, rows_of(f), :] = high
            mine = s_bf.at[r + 1, h, rows_of(f)]
            for dzl, dy in FRM_STEPS:
                remote(mine, mine, at + SHARE + h, (p, frm_at(dzl, dy))).start()
            if last:
                s_low[h, rows_of(f), :] = low
        if last:
            for h in range(SPLIT):
                mine = s_low.at[h, rows_of(f)]
                for dzl, dy in FRM_STEPS:
                    remote(mine, mine, at + LOW + h, (p, frm_at(dzl, dy))).start()

        numer_t = gram_t = 0.0
        for h in range(SPLIT):
            wait_bytes(s_bf.at[r + 1, h, pl.ds(0, COMP - ROWS)], recv_sem.at[at + SHARE + h])
            s_now = s_bf[r + 1, h]
            numer_t = numer_t + dot_nt(s_now, norm_t[h])
            gram_t = gram_t + dot_nt(s_now, s_now)
        mixed_part[r, :, pl.ds(0, FRM)] = numer_t.astype(BF16)
        mixed_part[r, :, pl.ds(FRM, COMP)] = gram_t.astype(BF16)
        remote(
            mixed_part.at[r, rows_of(1 - c, HALF)],
            core_in.at[r],
            at + CORE,
            pix_device(x, zh, 1 - c),
        ).start()
        wait_bytes(core_in.at[r], recv_sem.at[at + CORE])
        chip_sum = mixed_part[r, rows_of(c, HALF), :].astype(F32) + core_in[r].astype(F32)
        chip_part[r] = chip_sum.astype(BF16)
        for dx, dzh in CHIP_STEPS:
            ox, ozh, _ = pix_at(dx, dzh, 0)
            remote(
                chip_part.at[r, rows_of(ozh * 4 + ox)],
                chip_in.at[r, pix_block],
                at + CHIP,
                pix_device(ox, ozh, c),
            ).start()
        chip_in[r, pix_block] = chip_part[r, rows_of(pix_block), :]
        if last:
            for h in range(SPLIT):
                wait_bytes(s_low.at[h, pl.ds(0, COMP - ROWS)], recv_sem.at[at + LOW + h])
                whole = s_bf[r + 1, h].astype(F32) + s_low[h].astype(F32)
                s_wide[pl.ds(h * PART, PART), :] = whole.T
            pltpu.make_async_copy(s_wide, s_out, out_sem.at[0]).start()
        wait_bytes(chip_in.at[r, pl.ds(0, CHIPS - 1)], recv_sem.at[at + CHIP])
        total = summed(chip_in.at[r], CHIPS)
        (denom_t,) = product(
            total[:, FRM:], [t_bf[r]], t_block, [t_own[...]], [t_bf[r, rows_of(t_block), :]]
        )
        t_new = t_own[...] * total[:, :FRM] / (denom_t + epsilon)
        t_own[...] = t_new
        if not last:
            t_bf[r + 1, rows_of(t_block), :] = t_new.astype(BF16)
            mine = t_bf.at[r + 1, rows_of(t_block)]
            for dx, dzh, dc in PIX_STEPS:
                sem = at + (FAR if dzh else NEAR)
                remote(mine, mine, sem, pix_device(*pix_at(dx, dzh, dc))).start()
            for part, sem, count in ((0, NEAR, CHIPS - 1), (1, FAR, CHIPS)):
                wait_bytes(t_bf.at[r + 1, pl.ds(0, count * ROWS)], recv_sem.at[at + sem])
                if part:
                    send_gram(r + 1)
                group = lax.rem(zh + part, 2)
                spans = [pl.ds(pl.multiple_of(b * HALF + group * 64, 64), 64) for b in range(2)]
                t_rows = jnp.concatenate([t_bf[r + 1, span, :] for span in spans], axis=0)
                first = lax.rem(zl + group, 2)
                for h in range(SPLIT):
                    rows = dot_nn(t_rows, norm_t[h]).astype(BF16)
                    for b, span in enumerate(spans):
                        numer_part[r + 1, h, span, :] = rows[b * 64 : (b + 1) * 64]
                for h in range(SPLIT):
                    for i in (2, 0):
                        for dy in (2, 1, 3, 0):
                            other = frm_at(first + i, dy)
                            if i or dy:
                                send_numer(r + 1, h, [other])
                            else:

                                @pl.when(first > 0)
                                def _():
                                    send_numer(r + 1, h, [other])

            for h in range(SPLIT):
                numer_in[r + 1, h, f] = numer_part[r + 1, h, rows_of(f), :]
        else:
            t_wide[rows_of(t_block), :] = t_new
            mine = t_wide.at[rows_of(t_block)]
            for dx, dzh in CHIP_STEPS:
                ox, ozh, _ = pix_at(dx, dzh, 0)
                sem = at + (FAR if dzh else NEAR)
                remote(mine, mine, sem, pix_device(ox, ozh, c)).start()
            for part, sem, count in ((0, NEAR, 3), (1, FAR, 4)):
                wait_bytes(t_wide.at[pl.ds(0, count * ROWS)], recv_sem.at[at + sem])
                group = lax.rem(zh + part, 2)
                got = t_wide.at[pl.ds(pl.multiple_of(c * HALF + group * 64, 64), 64)]
                remote(got, got, at + RELAY + part, pix_device(x, zh, 1 - c)).start()
            for part in range(2):
                wait_bytes(t_wide.at[pl.ds(0, 64)], recv_sem.at[at + RELAY + part])
    result = pltpu.make_async_copy(t_wide, t_out, out_sem.at[1])
    result.start()

    @pl.when(has_right)
    def _():
        for copy in halos[0::2]:
            copy.wait_send()

    @pl.when(has_left)
    def _():
        for copy in halos[1::2]:
            copy.wait_send()

    for r in range(ROUNDS):
        last = r == ROUNDS - 1
        at = r * PHASES
        sent = [
            (GRAM, gram_in.at[r, pl.ds(0, GROUP - 1)]),
            (CORE_GRAM, gram_own.at[r, :, pl.ds(0, HALF)]),
            (CORE, core_in.at[r]),
            (CHIP, chip_in.at[r, pl.ds(0, CHIPS - 1)]),
        ]
        for h in range(SPLIT):
            sent.append((NUMER + h, numer_in.at[r, h, pl.ds(0, GROUP - 1)]))
            sent.append((SHARE + h, s_bf.at[r + 1, h, pl.ds(0, COMP - ROWS)]))
        if last:
            sent += [(LOW + h, s_low.at[h, pl.ds(0, COMP - ROWS)]) for h in range(SPLIT)]
            sent += [(NEAR, t_wide.at[pl.ds(0, 3 * ROWS)]), (FAR, t_wide.at[pl.ds(0, 4 * ROWS)])]
            sent += [(RELAY + part, t_wide.at[pl.ds(0, 64)]) for part in range(2)]
        else:
            sent += [
                (NEAR, t_bf.at[r + 1, pl.ds(0, 7 * ROWS)]),
                (FAR, t_bf.at[r + 1, pl.ds(0, 8 * ROWS)]),
            ]
        for sem, ref in sent:
            wait_bytes(ref, send_sem.at[at + sem])
    pltpu.make_async_copy(s_wide, s_out, out_sem.at[0]).wait()
    result.wait()


def hand_on(s_hbm, t_hbm, s_out, t_out, sem):
    copies = [
        pltpu.make_async_copy(s_hbm, s_out, sem.at[0]),
        pltpu.make_async_copy(t_hbm, t_out, sem.at[1]),
    ]
    for copy in copies:
        copy.start()
    for copy in copies:
        copy.wait()


def on_device(movie, taps, scale, base, spatial, temporal):
    hbm = pl.BlockSpec(memory_space=pltpu.HBM)
    shapes = (
        jax.ShapeDtypeStruct((PIX, COMP), F32),
        jax.ShapeDtypeStruct((COMP, FRM), F32),
    )
    s, t = pl.pallas_call(
        kernel,
        out_shape=shapes,
        in_specs=[hbm] * 6,
        out_specs=(hbm, hbm),
        scratch_shapes=[
            pltpu.VMEM((PIX, 2 * FRM), BF16),
            pltpu.VMEM((TAPS,), F32),
            pltpu.VMEM((PIX,), F32),
            pltpu.VMEM((PIX,), F32),
            pltpu.VMEM((PIX, COMP), F32),
            pltpu.VMEM((COMP, FRM), F32),
            pltpu.VMEM((1, 2 * FRM), F32),
            pltpu.VMEM((SPLIT, FRM, PART), BF16),
            pltpu.VMEM((SPLIT, COMP, PART), F32),
            pltpu.VMEM((SPLIT, ROWS, PART), F32),
            pltpu.VMEM((ROWS, FRM), F32),
            pltpu.VMEM((ROUNDS, COMP, FRM), BF16),
            pltpu.VMEM((ROUNDS, COMP, HALF), BF16),
            pltpu.VMEM((ROUNDS, GROUP, ROWS, HALF), BF16),
            pltpu.VMEM((ROUNDS, ROWS, COMP), F32),
            pltpu.VMEM((ROUNDS, SPLIT, COMP, PART), BF16),
            pltpu.VMEM((ROUNDS, SPLIT, GROUP, ROWS, PART), BF16),
            pltpu.VMEM((ROUNDS + 1, SPLIT, COMP, PART), BF16),
            pltpu.VMEM((SPLIT, COMP, PART), BF16),
            pltpu.VMEM((ROUNDS, COMP, FRM + COMP), BF16),
            pltpu.VMEM((ROUNDS, HALF, FRM + COMP), BF16),
            pltpu.VMEM((ROUNDS, HALF, FRM + COMP), BF16),
            pltpu.VMEM((ROUNDS, CHIPS, ROWS, FRM + COMP), BF16),
            pltpu.VMEM((PIX, COMP), F32),
            pltpu.VMEM((COMP, FRM), F32),
            pltpu.SemaphoreType.DMA((6,)),
            pltpu.SemaphoreType.DMA((2 * SPLIT,)),
            pltpu.SemaphoreType.DMA((2 * SPLIT,)),
            pltpu.SemaphoreType.DMA((ROUNDS * PHASES,)),
            pltpu.SemaphoreType.DMA((ROUNDS * PHASES,)),
            pltpu.SemaphoreType.DMA((2,)),
        ],
        compiler_params=pltpu.CompilerParams(
            collective_id=0, has_side_effects=True, vmem_limit_bytes=60 << 20
        ),
    )(movie, taps, scale, base, spatial, temporal)
    return pl.pallas_call(
        hand_on,
        out_shape=shapes,
        in_specs=[hbm, hbm],
        out_specs=(hbm, hbm),
        scratch_shapes=[pltpu.SemaphoreType.DMA((2,))],
        compiler_params=pltpu.CompilerParams(vmem_limit_bytes=60 << 20),
    )(s, t)


def solution(mesh):
    placed = (P("pix", "frm"), P(), P("pix"), P("pix"), P("pix", None), P(None, "frm"))
    return jax.shard_map(
        on_device,
        mesh=mesh,
        in_specs=placed,
        out_specs=(P("pix", None), P(None, "frm")),
        check_vma=False,
    )
```

```python
import functools

import jax
import jax.numpy as jnp
from jax import lax
from jax.experimental import pallas as pl
from jax.experimental.pallas import tpu as pltpu
from jax.sharding import PartitionSpec as P

ROUNDS = 2
MESH = pl.DeviceIdType.MESH
F32 = jnp.float32
BF16 = jnp.bfloat16
epsilon = 1e-06

GROUP = 16
CHIPS = 8
PIX = 512
FRM = 256
COMP = 256
ROWS = COMP // GROUP
HALO = 128
SPLIT = 2
PART = PIX // SPLIT
HALF = COMP // 2
TAPS = 257


def far_first(steps, hops):
    return sorted(steps, key=lambda step: -hops(*step))


FRM_STEPS = far_first(
    [(dzl, dy) for dzl in range(4) for dy in range(4) if dzl or dy],
    lambda dzl, dy: dzl + min(dy, 4 - dy),
)
CHIP_STEPS = far_first(
    [(dx, dzh) for dx in range(4) for dzh in range(2) if dx or dzh],
    lambda dx, dzh: min(dx, 4 - dx) + 4 * dzh,
)
PIX_STEPS = far_first(
    [(dx, dzh, dc) for dx in range(4) for dzh in range(2) for dc in range(2) if dx or dzh or dc],
    lambda dx, dzh, dc: min(dx, 4 - dx) + 4 * dzh + 0.5 * dc,
)


def dot_nn(a, b):
    return lax.dot_general(a, b, (((1,), (0,)), ((), ())), preferred_element_type=F32)


def dot_nt(a, b):
    return lax.dot_general(a, b, (((1,), (1,)), ((), ())), preferred_element_type=F32)


def split(value):
    high = value.astype(BF16)
    return high, (value - high.astype(F32)).astype(BF16)


def product(gram, wholes, block, owns, own_copies):
    terms = jnp.concatenate(split(gram), axis=0)
    row = lax.broadcasted_iota(jnp.int32, gram.shape, 0)
    column = lax.broadcasted_iota(jnp.int32, gram.shape, 1)
    diagonal = jnp.sum(jnp.where(column == row + block * ROWS, gram, 0.0), axis=1, keepdims=True)
    results = []
    for whole, own, copy in zip(wholes, owns, own_copies):
        both = dot_nn(terms, whole)
        results.append(both[:ROWS] + both[ROWS:] + diagonal * (own - copy.astype(F32)))
    return results


def rows_of(index, count=ROWS):
    return pl.ds(pl.multiple_of(index * count, count), count)


def wait_bytes(ref, sem):
    pltpu.make_async_copy(ref, ref, sem).wait()


def summed(inbox, count):
    total = inbox[0].astype(F32)
    for slot in range(1, count):
        total = total + inbox[slot].astype(F32)
    return total


NUMER, GRAM, SHARE, LOW, CORE_GRAM, CORE, CHIP, NEAR, FAR, RELAY = 0, 2, 3, 5, 7, 8, 9, 10, 11, 12
PHASES = 14


def kernel(
    movie_hbm, taps_hbm, scale_hbm, base_hbm, spatial_hbm, temporal_hbm,
    s_out, t_out,
    padded, taps_v, scale_v, base_v, spatial_v, temporal_v,
    coef, norm_t, s_zero_t, s_own, t_own, t_bf,
    gram_part, gram_in, gram_own, numer_part, numer_in, s_bf, s_low,
    mixed_part, core_in, chip_part, chip_in,
    load_sem, halo_send, halo_recv, send_sem, recv_sem, met,
):
    p = lax.axis_index("pix")
    f = lax.axis_index("frm")
    x, zh, c = lax.div(p, 4), lax.rem(lax.div(p, 2), 2), lax.rem(p, 2)
    zl, y = lax.div(f, 4), lax.rem(f, 4)
    pix_block = zh * 4 + x
    t_block = c * CHIPS + pix_block

    def pix_at(dx, dzh, dc):
        return lax.rem(x + dx, 4), lax.rem(zh + dzh, 2), lax.rem(c + dc, 2)

    def pix_device(ox, ozh, oc):
        return ((ox * 2 + ozh) * 2 + oc, f)

    def frm_at(dzl, dy):
        return lax.rem(zl + dzl, 4) * 4 + lax.rem(y + dy, 4)

    barrier = pltpu.get_barrier_semaphore()
    x_line = [pix_device(*pix_at(dx, 0, 0)) for dx in (2, 1, 3)]
    z_far, partner = pix_device(x, 1 - zh, c), pix_device(x, zh, 1 - c)
    z_line = [(p, frm_at(dzl, 0)) for dzl in (3, 2, 1)]
    y_line = [(p, frm_at(0, dy)) for dy in (2, 1, 3)]

    def signal(sem, targets):
        for target in targets:
            pl.semaphore_signal(sem, inc=1, device_id=target, device_id_type=MESH)

    greeted = [z_far, *z_line, *x_line, *y_line, partner]
    signal(barrier, greeted)
    corner_right = jnp.logical_and(y == 3, f < GROUP - 1)
    corner_left = jnp.logical_and(y == 0, f > 0)

    @pl.when(corner_right)
    def _():
        signal(barrier, [(p, f + 1)])

    @pl.when(corner_left)
    def _():
        signal(barrier, [(p, f - 1)])

    loads = [
        pltpu.make_async_copy(src, dst, load_sem.at[i])
        for i, (src, dst) in enumerate(
            (
                (movie_hbm, padded.at[:, pl.ds(HALO, FRM)]),
                (temporal_hbm, temporal_v),
                (spatial_hbm, spatial_v),
                (taps_hbm, taps_v),
                (scale_hbm, scale_v),
                (base_hbm, base_v),
            )
        )
    ]
    for copy in loads:
        copy.start()

    def remote(src, dst, sem, target):
        return pltpu.make_async_remote_copy(
            src_ref=src,
            dst_ref=dst,
            send_sem=send_sem.at[sem],
            recv_sem=recv_sem.at[sem],
            device_id=target,
            device_id_type=MESH,
        )

    cornered = jnp.logical_or(corner_right, corner_left)

    @pl.when(cornered)
    def _():
        pl.semaphore_wait(barrier, len(greeted) + 1)

    @pl.when(jnp.logical_not(cornered))
    def _():
        pl.semaphore_wait(barrier, len(greeted))

    met_frm, met_pix, met_core = (met.at[i] for i in range(3))
    loads[0].wait()
    halos = []
    for h in range(SPLIT):
        pixels = pl.ds(h * PART, PART)
        for side, (source, target, step) in enumerate(
            ((FRM, 0, 1), (HALO, HALO + FRM, GROUP - 1))
        ):
            halos.append(
                pltpu.make_async_remote_copy(
                    src_ref=padded.at[pixels, pl.ds(source, HALO)],
                    dst_ref=padded.at[pixels, pl.ds(target, HALO)],
                    send_sem=halo_send.at[2 * h + side],
                    recv_sem=halo_recv.at[2 * h + side],
                    device_id=(p, lax.rem(f + step, GROUP)),
                    device_id_type=MESH,
                )
            )
    has_right, has_left = f < GROUP - 1, f > 0

    @pl.when(has_right)
    def _():
        for copy in halos[0::2]:
            copy.start()

    @pl.when(has_left)
    def _():
        for copy in halos[1::2]:
            copy.start()

    signal(met_frm, z_line)
    signal(met_pix, [z_far, *x_line, partner])

    def make_gram(r):
        t_now = t_bf[r]
        t_half = t_bf[r, rows_of(c, HALF), :]
        gram_part[r] = dot_nt(t_now, t_half).astype(BF16)

    def send_gram(r):
        for dzl, dy in FRM_STEPS:
            other = frm_at(dzl, dy)
            remote(
                gram_part.at[r, rows_of(other)], gram_in.at[r, f], r * PHASES + GRAM, (p, other)
            ).start()
        gram_in[r, f] = gram_part[r, rows_of(f), :]

    def finish_gram(r):
        wait_bytes(gram_in.at[r, pl.ds(0, GROUP - 1)], recv_sem.at[r * PHASES + GRAM])
        half = pl.ds(pl.multiple_of(c * HALF, HALF), HALF)
        gram_own[r, :, half] = summed(gram_in.at[r], GROUP)
        mine = gram_own.at[r, :, half]
        copy = remote(mine, mine, r * PHASES + CORE_GRAM, pix_device(x, zh, 1 - c))
        copy.start()
        copy.wait_recv()

    loads[1].wait()
    t_bf[0] = temporal_v[...].astype(BF16)
    make_gram(0)
    pl.semaphore_wait(met_frm, len(z_line))
    send_gram(0)

    @pl.when(f == 0)
    def _():
        padded[:, pl.ds(0, HALO)] = jnp.zeros((PIX, HALO), BF16)

    @pl.when(f == GROUP - 1)
    def _():
        padded[:, pl.ds(HALO + FRM, HALO)] = jnp.zeros((PIX, HALO), BF16)

    for copy in loads[2:]:
        copy.wait()
    coef[...] = jnp.zeros_like(coef)
    centre = lax.broadcasted_iota(jnp.int32, (1, TAPS), 1) == HALO
    coef[:, pl.ds(0, TAPS)] = jnp.where(centre, 1.0, 0.0).astype(F32) - taps_v[...][None]
    band_t = pltpu.roll(
        jnp.broadcast_to(coef[...], (FRM, 2 * FRM)), 0, 1, stride=1, stride_axis=0
    ).astype(BF16)
    spatial_t = spatial_v[...].T
    for h in range(SPLIT):
        s_zero_t[h] = spatial_t[:, h * PART : (h + 1) * PART]
        s_bf[0, h] = s_zero_t[h].astype(BF16)
        s_own[h] = s_zero_t[h, rows_of(f), :]
    t_own[...] = temporal_v[rows_of(t_block), :]
    pl.semaphore_wait(met_pix, 2 + len(x_line))
    signal(met_core, [partner])

    def send_numer(r, h, others):
        for other in others:
            remote(
                numer_part.at[r, h, rows_of(other)],
                numer_in.at[r, h, f],
                r * PHASES + NUMER + h,
                (p, other),
            ).start()

    for h in range(SPLIT):
        pixels = pl.ds(h * PART, PART)

        @pl.when(has_left)
        def _():
            halos[2 * h].wait_recv()

        @pl.when(has_right)
        def _():
            halos[2 * h + 1].wait_recv()

        mixed = dot_nt(band_t, padded[pixels, :])
        scaled = scale_v[pixels][None] * mixed + base_v[pixels][None]
        norm_t[h] = jnp.maximum(scaled, 0.0).astype(BF16)
        numer_part[0, h] = dot_nn(t_bf[0], norm_t[h]).astype(BF16)
        send_numer(0, h, [frm_at(dzl, dy) for dzl, dy in FRM_STEPS])
        numer_in[0, h, f] = numer_part[0, h, rows_of(f), :]

    for r in range(ROUNDS):
        last = r == ROUNDS - 1
        at = r * PHASES
        finish_gram(r)
        denoms = product(
            gram_own[r],
            [s_bf[r, h] for h in range(SPLIT)],
            f,
            [s_own[h] for h in range(SPLIT)],
            [s_bf[r, h, rows_of(f), :] for h in range(SPLIT)],
        )
        for h in range(SPLIT):
            wait_bytes(numer_in.at[r, h, pl.ds(0, GROUP - 1)], recv_sem.at[at + NUMER + h])
            numer = summed(numer_in.at[r, h], GROUP)
            s_new = s_own[h] * numer / (denoms[h] + epsilon)
            s_own[h] = s_new
            high, low = split(s_new)
            s_bf[r + 1, h, rows_of(f), :] = high
            mine = s_bf.at[r + 1, h, rows_of(f)]
            for dzl, dy in FRM_STEPS:
                remote(mine, mine, at + SHARE + h, (p, frm_at(dzl, dy))).start()
            if last:
                s_low[h, rows_of(f), :] = low

        numer_t = gram_t = 0.0
        for h in range(SPLIT):
            wait_bytes(s_bf.at[r + 1, h, pl.ds(0, COMP - ROWS)], recv_sem.at[at + SHARE + h])
            s_now = s_bf[r + 1, h]
            numer_t = numer_t + dot_nt(s_now, norm_t[h])
            gram_t = gram_t + dot_nt(s_now, s_now)
        mixed_part[r, :, pl.ds(0, FRM)] = numer_t.astype(BF16)
        mixed_part[r, :, pl.ds(FRM, COMP)] = gram_t.astype(BF16)
        remote(
            mixed_part.at[r, rows_of(1 - c, HALF)],
            core_in.at[r],
            at + CORE,
            pix_device(x, zh, 1 - c),
        ).start()
        wait_bytes(core_in.at[r], recv_sem.at[at + CORE])
        chip_sum = mixed_part[r, rows_of(c, HALF), :].astype(F32) + core_in[r].astype(F32)
        chip_part[r] = chip_sum.astype(BF16)
        if not r:
            pl.semaphore_wait(met_core, 1)
        for dx, dzh in CHIP_STEPS:
            ox, ozh, _ = pix_at(dx, dzh, 0)
            remote(
                chip_part.at[r, rows_of(ozh * 4 + ox)],
                chip_in.at[r, pix_block],
                at + CHIP,
                pix_device(ox, ozh, c),
            ).start()
        chip_in[r, pix_block] = chip_part[r, rows_of(pix_block), :]
        if last:
            for h in range(SPLIT):
                mine = s_low.at[h, rows_of(f)]
                for dzl, dy in FRM_STEPS:
                    remote(mine, mine, at + LOW + h, (p, frm_at(dzl, dy))).start()
        wait_bytes(chip_in.at[r, pl.ds(0, CHIPS - 1)], recv_sem.at[at + CHIP])
        total = summed(chip_in.at[r], CHIPS)
        (denom_t,) = product(
            total[:, FRM:], [t_bf[r]], t_block, [t_own[...]], [t_bf[r, rows_of(t_block), :]]
        )
        t_new = t_own[...] * total[:, :FRM] / (denom_t + epsilon)
        t_own[...] = t_new
        if not last:
            t_bf[r + 1, rows_of(t_block), :] = t_new.astype(BF16)
            mine = t_bf.at[r + 1, rows_of(t_block)]
            for dx, dzh, dc in PIX_STEPS:
                sem = at + (FAR if dzh else NEAR)
                remote(mine, mine, sem, pix_device(*pix_at(dx, dzh, dc))).start()
            for part, sem, count in ((0, NEAR, CHIPS - 1), (1, FAR, CHIPS)):
                wait_bytes(t_bf.at[r + 1, pl.ds(0, count * ROWS)], recv_sem.at[at + sem])
                if part:
                    make_gram(r + 1)
                    send_gram(r + 1)
                group = lax.rem(zh + part, 2)
                spans = [pl.ds(pl.multiple_of(b * HALF + group * 64, 64), 64) for b in range(2)]
                t_rows = jnp.concatenate([t_bf[r + 1, span, :] for span in spans], axis=0)
                first = lax.rem(zl + group, 2)
                for h in range(SPLIT):
                    rows = dot_nn(t_rows, norm_t[h]).astype(BF16)
                    for b, span in enumerate(spans):
                        numer_part[r + 1, h, span, :] = rows[b * 64 : (b + 1) * 64]
                for h in range(SPLIT):
                    for i in (2, 0):
                        for dy in (2, 1, 3, 0):
                            other = frm_at(first + i, dy)
                            if i or dy:
                                send_numer(r + 1, h, [other])
                            else:

                                @pl.when(first > 0)
                                def _():
                                    send_numer(r + 1, h, [other])

            for h in range(SPLIT):
                numer_in[r + 1, h, f] = numer_part[r + 1, h, rows_of(f), :]
        else:
            t_out[rows_of(t_block), :] = t_new
            mine = t_out.at[rows_of(t_block)]
            for dx, dzh in CHIP_STEPS:
                ox, ozh, _ = pix_at(dx, dzh, 0)
                sem = at + (FAR if dzh else NEAR)
                remote(mine, mine, sem, pix_device(ox, ozh, c)).start()
            for h in range(SPLIT):
                wait_bytes(s_low.at[h, pl.ds(0, COMP - ROWS)], recv_sem.at[at + LOW + h])
                whole = s_bf[r + 1, h].astype(F32) + s_low[h].astype(F32)
                s_out[pl.ds(h * PART, PART), :] = whole.T
            for part, sem, count in ((0, NEAR, 3), (1, FAR, 4)):
                wait_bytes(t_out.at[pl.ds(0, count * ROWS)], recv_sem.at[at + sem])
                group = lax.rem(zh + part, 2)
                got = t_out.at[pl.ds(pl.multiple_of(c * HALF + group * 64, 64), 64)]
                remote(got, got, at + RELAY + part, pix_device(x, zh, 1 - c)).start()
            for part in range(2):
                wait_bytes(t_out.at[pl.ds(0, 64)], recv_sem.at[at + RELAY + part])

    @pl.when(has_right)
    def _():
        for copy in halos[0::2]:
            copy.wait_send()

    @pl.when(has_left)
    def _():
        for copy in halos[1::2]:
            copy.wait_send()

    for r in range(ROUNDS):
        last = r == ROUNDS - 1
        at = r * PHASES
        sent = [
            (GRAM, gram_in.at[r, pl.ds(0, GROUP - 1)]),
            (CORE_GRAM, gram_own.at[r, :, pl.ds(0, HALF)]),
            (CORE, core_in.at[r]),
            (CHIP, chip_in.at[r, pl.ds(0, CHIPS - 1)]),
        ]
        for h in range(SPLIT):
            sent.append((NUMER + h, numer_in.at[r, h, pl.ds(0, GROUP - 1)]))
            sent.append((SHARE + h, s_bf.at[r + 1, h, pl.ds(0, COMP - ROWS)]))
        if last:
            sent += [(LOW + h, s_low.at[h, pl.ds(0, COMP - ROWS)]) for h in range(SPLIT)]
            sent += [(NEAR, t_out.at[pl.ds(0, 3 * ROWS)]), (FAR, t_out.at[pl.ds(0, 4 * ROWS)])]
            sent += [(RELAY + part, t_out.at[pl.ds(0, 64)]) for part in range(2)]
        else:
            sent += [
                (NEAR, t_bf.at[r + 1, pl.ds(0, 7 * ROWS)]),
                (FAR, t_bf.at[r + 1, pl.ds(0, 8 * ROWS)]),
            ]
        for sem, ref in sent:
            wait_bytes(ref, send_sem.at[at + sem])


def hand_on(s_v, t_v, s_out, t_out, sem):
    copies = [
        pltpu.make_async_copy(s_v, s_out, sem.at[0]),
        pltpu.make_async_copy(t_v, t_out, sem.at[1]),
    ]
    for copy in copies:
        copy.start()
    for copy in copies:
        copy.wait()


def on_device(movie, taps, scale, base, spatial, temporal):
    hbm = pl.BlockSpec(memory_space=pltpu.HBM)
    vmem = pl.BlockSpec(memory_space=pltpu.VMEM)
    shapes = (
        jax.ShapeDtypeStruct((PIX, COMP), F32),
        jax.ShapeDtypeStruct((COMP, FRM), F32),
    )
    operands = [
        pltpu.with_memory_space_constraint(array, pltpu.HBM)
        for array in (movie, taps, scale, base, spatial, temporal)
    ]
    s, t = pl.pallas_call(
        kernel,
        out_shape=shapes,
        in_specs=[hbm] * 6,
        out_specs=(vmem, vmem),
        scratch_shapes=[
            pltpu.VMEM((PIX, 2 * FRM), BF16),
            pltpu.VMEM((TAPS,), F32),
            pltpu.VMEM((PIX,), F32),
            pltpu.VMEM((PIX,), F32),
            pltpu.VMEM((PIX, COMP), F32),
            pltpu.VMEM((COMP, FRM), F32),
            pltpu.VMEM((1, 2 * FRM), F32),
            pltpu.VMEM((SPLIT, FRM, PART), BF16),
            pltpu.VMEM((SPLIT, COMP, PART), F32),
            pltpu.VMEM((SPLIT, ROWS, PART), F32),
            pltpu.VMEM((ROWS, FRM), F32),
            pltpu.VMEM((ROUNDS, COMP, FRM), BF16),
            pltpu.VMEM((ROUNDS, COMP, HALF), BF16),
            pltpu.VMEM((ROUNDS, GROUP, ROWS, HALF), BF16),
            pltpu.VMEM((ROUNDS, ROWS, COMP), F32),
            pltpu.VMEM((ROUNDS, SPLIT, COMP, PART), BF16),
            pltpu.VMEM((ROUNDS, SPLIT, GROUP, ROWS, PART), BF16),
            pltpu.VMEM((ROUNDS + 1, SPLIT, COMP, PART), BF16),
            pltpu.VMEM((SPLIT, COMP, PART), BF16),
            pltpu.VMEM((ROUNDS, COMP, FRM + COMP), BF16),
            pltpu.VMEM((ROUNDS, HALF, FRM + COMP), BF16),
            pltpu.VMEM((ROUNDS, HALF, FRM + COMP), BF16),
            pltpu.VMEM((ROUNDS, CHIPS, ROWS, FRM + COMP), BF16),
            pltpu.SemaphoreType.DMA((6,)),
            pltpu.SemaphoreType.DMA((2 * SPLIT,)),
            pltpu.SemaphoreType.DMA((2 * SPLIT,)),
            pltpu.SemaphoreType.DMA((ROUNDS * PHASES,)),
            pltpu.SemaphoreType.DMA((ROUNDS * PHASES,)),
            pltpu.SemaphoreType.REGULAR((3,)),
        ],
        compiler_params=pltpu.CompilerParams(
            collective_id=0, has_side_effects=True, vmem_limit_bytes=40 << 20
        ),
    )(*operands)
    return pl.pallas_call(
        hand_on,
        out_shape=shapes,
        in_specs=[vmem, vmem],
        out_specs=(hbm, hbm),
        scratch_shapes=[pltpu.SemaphoreType.DMA((2,))],
        compiler_params=pltpu.CompilerParams(vmem_limit_bytes=40 << 20),
    )(s, t)


def solution(mesh):
    placed = (P("pix", "frm"), P(), P("pix"), P("pix"), P("pix", None), P(None, "frm"))
    return jax.shard_map(
        on_device,
        mesh=mesh,
        in_specs=placed,
        out_specs=(P("pix", None), P(None, "frm")),
        check_vma=False,
    )
```

```python
import functools

import jax
import jax.numpy as jnp
from jax import lax
from jax.experimental import pallas as pl
from jax.experimental.pallas import tpu as pltpu
from jax.sharding import PartitionSpec as P

ROUNDS = 2
MESH = pl.DeviceIdType.MESH
F32 = jnp.float32
BF16 = jnp.bfloat16
epsilon = 1e-06

GROUP = 16
CHIPS = 8
PIX = 512
FRM = 256
COMP = 256
ROWS = COMP // GROUP
HALO = 128
SPLIT = 2
PART = PIX // SPLIT
HALF = COMP // 2
TAPS = 257


def far_first(steps, hops):
    return sorted(steps, key=lambda step: -hops(*step))


FRM_STEPS = far_first(
    [(dzl, dy) for dzl in range(4) for dy in range(4) if dzl or dy],
    lambda dzl, dy: dzl + min(dy, 4 - dy),
)
CHIP_STEPS = far_first(
    [(dx, dzh) for dx in range(4) for dzh in range(2) if dx or dzh],
    lambda dx, dzh: min(dx, 4 - dx) + 4 * dzh,
)
PIX_STEPS = far_first(
    [(dx, dzh, dc) for dx in range(4) for dzh in range(2) for dc in range(2) if dx or dzh or dc],
    lambda dx, dzh, dc: min(dx, 4 - dx) + 4 * dzh + 0.5 * dc,
)


def dot_nn(a, b):
    return lax.dot_general(a, b, (((1,), (0,)), ((), ())), preferred_element_type=F32)


def dot_nt(a, b):
    return lax.dot_general(a, b, (((1,), (1,)), ((), ())), preferred_element_type=F32)


def split(value):
    high = value.astype(BF16)
    return high, (value - high.astype(F32)).astype(BF16)


def product(gram, wholes, block, owns, own_copies):
    terms = jnp.concatenate(split(gram), axis=0)
    row = lax.broadcasted_iota(jnp.int32, gram.shape, 0)
    column = lax.broadcasted_iota(jnp.int32, gram.shape, 1)
    diagonal = jnp.sum(jnp.where(column == row + block * ROWS, gram, 0.0), axis=1, keepdims=True)
    results = []
    for whole, own, copy in zip(wholes, owns, own_copies):
        both = dot_nn(terms, whole)
        results.append(both[:ROWS] + both[ROWS:] + diagonal * (own - copy.astype(F32)))
    return results


def rows_of(index, count=ROWS):
    return pl.ds(pl.multiple_of(index * count, count), count)


def wait_bytes(ref, sem):
    pltpu.make_async_copy(ref, ref, sem).wait()


def summed(inbox, count):
    total = inbox[0].astype(F32)
    for slot in range(1, count):
        total = total + inbox[slot].astype(F32)
    return total


NUMER, GRAM, SHARE, LOW, CORE_GRAM, CORE, CHIP, NEAR, FAR, RELAY = 0, 2, 3, 5, 7, 8, 9, 10, 11, 12
ACROSS = 14
PHASES = 15


def kernel(
    movie_hbm, taps_hbm, scale_hbm, base_hbm, spatial_hbm, temporal_hbm,
    s_out, t_out,
    padded, taps_v, scale_v, base_v, spatial_v, temporal_v,
    coef, norm_t, s_zero_t, s_own, t_own, t_across, t_bf, t_turned,
    gram_part, gram_in, gram_own, numer_part, numer_in, s_bf, s_low,
    mixed_part, core_in, chip_part, chip_in,
    load_sem, halo_send, halo_recv, send_sem, recv_sem, met,
):
    p = lax.axis_index("pix")
    f = lax.axis_index("frm")
    x, zh, c = lax.div(p, 4), lax.rem(lax.div(p, 2), 2), lax.rem(p, 2)
    zl, y = lax.div(f, 4), lax.rem(f, 4)
    pix_block = zh * 4 + x
    t_block = c * CHIPS + pix_block

    def pix_at(dx, dzh, dc):
        return lax.rem(x + dx, 4), lax.rem(zh + dzh, 2), lax.rem(c + dc, 2)

    def pix_device(ox, ozh, oc):
        return ((ox * 2 + ozh) * 2 + oc, f)

    def frm_at(dzl, dy):
        return lax.rem(zl + dzl, 4) * 4 + lax.rem(y + dy, 4)

    barrier = pltpu.get_barrier_semaphore()
    x_line = [pix_device(*pix_at(dx, 0, 0)) for dx in (2, 1, 3)]
    partner = pix_device(x, zh, 1 - c)
    z_two = [(pix_device(x, 1 - zh, c)[0], frm_at(2, 0)), (p, frm_at(2, 0))]
    z_line = [(p, frm_at(dzl, 0)) for dzl in (3, 2, 1)]
    y_line = [(p, frm_at(0, dy)) for dy in (2, 1, 3)]

    def signal(sem, targets):
        for target in targets:
            pl.semaphore_signal(sem, inc=1, device_id=target, device_id_type=MESH)

    greeted = [*z_line, z_two[0], *x_line, *y_line, partner]
    signal(barrier, greeted)
    corner_right = jnp.logical_and(y == 3, f < GROUP - 1)
    corner_left = jnp.logical_and(y == 0, f > 0)

    @pl.when(corner_right)
    def _():
        signal(barrier, [(p, f + 1)])

    @pl.when(corner_left)
    def _():
        signal(barrier, [(p, f - 1)])

    loads = [
        pltpu.make_async_copy(src, dst, load_sem.at[i])
        for i, (src, dst) in enumerate(
            (
                (movie_hbm, padded.at[:, pl.ds(HALO, FRM)]),
                (temporal_hbm, temporal_v),
                (spatial_hbm, spatial_v),
                (taps_hbm, taps_v),
                (scale_hbm, scale_v),
                (base_hbm, base_v),
            )
        )
    ]
    for copy in loads:
        copy.start()

    def remote(src, dst, sem, target):
        return pltpu.make_async_remote_copy(
            src_ref=src,
            dst_ref=dst,
            send_sem=send_sem.at[sem],
            recv_sem=recv_sem.at[sem],
            device_id=target,
            device_id_type=MESH,
        )

    cornered = jnp.logical_or(corner_right, corner_left)

    @pl.when(cornered)
    def _():
        pl.semaphore_wait(barrier, len(greeted) + 1)

    @pl.when(jnp.logical_not(cornered))
    def _():
        pl.semaphore_wait(barrier, len(greeted))

    met_frm, met_two, met_line, met_pix = (met.at[i] for i in range(4))
    loads[0].wait()
    halos = []
    for h in range(SPLIT):
        pixels = pl.ds(h * PART, PART)
        for side, (source, target, step) in enumerate(
            ((FRM, 0, 1), (HALO, HALO + FRM, GROUP - 1))
        ):
            halos.append(
                pltpu.make_async_remote_copy(
                    src_ref=padded.at[pixels, pl.ds(source, HALO)],
                    dst_ref=padded.at[pixels, pl.ds(target, HALO)],
                    send_sem=halo_send.at[2 * h + side],
                    recv_sem=halo_recv.at[2 * h + side],
                    device_id=(p, lax.rem(f + step, GROUP)),
                    device_id_type=MESH,
                )
            )
    has_right, has_left = f < GROUP - 1, f > 0

    @pl.when(has_right)
    def _():
        for copy in halos[0::2]:
            copy.start()

    @pl.when(has_left)
    def _():
        for copy in halos[1::2]:
            copy.start()

    signal(met_frm, z_line)
    signal(met_two, [*z_two, *x_line, partner])

    def make_gram(r):
        t_now = t_bf[r]
        t_half = t_bf[r, rows_of(c, HALF), :]
        gram_part[r] = dot_nt(t_now, t_half).astype(BF16)

    def send_gram(r):
        for dzl, dy in FRM_STEPS:
            other = frm_at(dzl, dy)
            remote(
                gram_part.at[r, rows_of(other)], gram_in.at[r, f], r * PHASES + GRAM, (p, other)
            ).start()
        gram_in[r, f] = gram_part[r, rows_of(f), :]

    def finish_gram(r):
        wait_bytes(gram_in.at[r, pl.ds(0, GROUP - 1)], recv_sem.at[r * PHASES + GRAM])
        half = pl.ds(pl.multiple_of(c * HALF, HALF), HALF)
        gram_own[r, :, half] = summed(gram_in.at[r], GROUP)
        mine = gram_own.at[r, :, half]
        copy = remote(mine, mine, r * PHASES + CORE_GRAM, pix_device(x, zh, 1 - c))
        copy.start()
        copy.wait_recv()

    loads[1].wait()
    t_bf[0] = temporal_v[...].astype(BF16)
    make_gram(0)
    pl.semaphore_wait(met_frm, len(z_line))
    send_gram(0)

    @pl.when(f == 0)
    def _():
        padded[:, pl.ds(0, HALO)] = jnp.zeros((PIX, HALO), BF16)

    @pl.when(f == GROUP - 1)
    def _():
        padded[:, pl.ds(HALO + FRM, HALO)] = jnp.zeros((PIX, HALO), BF16)

    for copy in loads[2:]:
        copy.wait()
    coef[...] = jnp.zeros_like(coef)
    centre = lax.broadcasted_iota(jnp.int32, (1, TAPS), 1) == HALO
    coef[:, pl.ds(0, TAPS)] = jnp.where(centre, 1.0, 0.0).astype(F32) - taps_v[...][None]
    band_t = pltpu.roll(
        jnp.broadcast_to(coef[...], (FRM, 2 * FRM)), 0, 1, stride=1, stride_axis=0
    ).astype(BF16)
    spatial_t = spatial_v[...].T
    for h in range(SPLIT):
        s_zero_t[h] = spatial_t[:, h * PART : (h + 1) * PART]
        s_bf[0, h] = s_zero_t[h].astype(BF16)
        s_own[h] = s_zero_t[h, rows_of(f), :]
    t_own[...] = temporal_v[rows_of(t_block), :]
    pl.semaphore_wait(met_two, len(z_two) + len(x_line) + 1)
    signal(met_line, [*x_line, partner])

    def send_numer(r, h, others):
        for other in others:
            remote(
                numer_part.at[r, h, rows_of(other)],
                numer_in.at[r, h, f],
                r * PHASES + NUMER + h,
                (p, other),
            ).start()

    for h in range(SPLIT):
        pixels = pl.ds(h * PART, PART)

        @pl.when(has_left)
        def _():
            halos[2 * h].wait_recv()

        @pl.when(has_right)
        def _():
            halos[2 * h + 1].wait_recv()

        mixed = dot_nt(band_t, padded[pixels, :])
        scaled = scale_v[pixels][None] * mixed + base_v[pixels][None]
        norm_t[h] = jnp.maximum(scaled, 0.0).astype(BF16)
        numer_part[0, h] = dot_nn(t_bf[0], norm_t[h]).astype(BF16)
        send_numer(0, h, [frm_at(dzl, dy) for dzl, dy in FRM_STEPS])
        numer_in[0, h, f] = numer_part[0, h, rows_of(f), :]

    chips, ends = [], []
    for dx, dzh in CHIP_STEPS:
        ox, ozh, _ = pix_at(dx, dzh, 0)
        chips.append((ox, ozh, pix_device(ox, ozh, c)))
    for dx in (2, 1, 3, 0):
        for ozh in range(2):
            ox = lax.rem(x + dx, 4)
            ends.append((ox, ozh, ((ox * 2 + ozh) * 2 + c, frm_at(2, 0))))

    pl.semaphore_wait(met_line, len(x_line) + 1)
    signal(met_pix, [partner])

    for r in range(ROUNDS):
        last = r == ROUNDS - 1
        at = r * PHASES
        finish_gram(r)
        denoms = product(
            gram_own[r],
            [s_bf[r, h] for h in range(SPLIT)],
            f,
            [s_own[h] for h in range(SPLIT)],
            [s_bf[r, h, rows_of(f), :] for h in range(SPLIT)],
        )
        for h in range(SPLIT):
            wait_bytes(numer_in.at[r, h, pl.ds(0, GROUP - 1)], recv_sem.at[at + NUMER + h])
            numer = summed(numer_in.at[r, h], GROUP)
            s_new = s_own[h] * numer / (denoms[h] + epsilon)
            s_own[h] = s_new
            high, low = split(s_new)
            s_bf[r + 1, h, rows_of(f), :] = high
            mine = s_bf.at[r + 1, h, rows_of(f)]
            for dzl, dy in FRM_STEPS:
                remote(mine, mine, at + SHARE + h, (p, frm_at(dzl, dy))).start()
            if last:
                s_low[y, zl, :, pl.ds(h * PART, PART)] = low

        if last:
            for target in z_line:
                remote(s_low.at[y, zl], s_low.at[y, zl], at + LOW, target).start()

        numer_t = second_t = 0.0
        for h in range(SPLIT):
            wait_bytes(s_bf.at[r + 1, h, pl.ds(0, COMP - ROWS)], recv_sem.at[at + SHARE + h])
            s_now = s_bf[r + 1, h]
            numer_t = numer_t + dot_nt(s_now, norm_t[h])
            if last:
                second = dot_nn(t_turned[...], s_now).astype(BF16)
            else:
                second = s_now
            second_t = second_t + dot_nt(s_now, second)
        mixed_part[r, :, pl.ds(0, FRM)] = numer_t.astype(BF16)
        mixed_part[r, :, pl.ds(FRM, COMP)] = second_t.astype(BF16)
        remote(
            mixed_part.at[r, rows_of(1 - c, HALF)],
            core_in.at[r],
            at + CORE,
            pix_device(x, zh, 1 - c),
        ).start()
        wait_bytes(core_in.at[r], recv_sem.at[at + CORE])
        chip_sum = mixed_part[r, rows_of(c, HALF), :].astype(F32) + core_in[r].astype(F32)
        chip_part[r] = chip_sum.astype(BF16)
        if not r:
            pl.semaphore_wait(met_pix, 1)
        for ox, ozh, target in ends if last else chips:
            remote(
                chip_part.at[r, rows_of(ozh * 4 + ox)],
                chip_in.at[r, pix_block],
                at + CHIP,
                target,
            ).start()
        if last:
            wait_bytes(s_low.at[0, pl.ds(0, 3)], recv_sem.at[at + LOW])
            for target in y_line:
                remote(s_low.at[y], s_low.at[y], at + LOW + 1, target).start()
        if not last:
            chip_in[r, pix_block] = chip_part[r, rows_of(pix_block), :]
            wait_bytes(chip_in.at[r, pl.ds(0, CHIPS - 1)], recv_sem.at[at + CHIP])
            total = summed(chip_in.at[r], CHIPS)
            (denom_t,) = product(
                total[:, FRM:], [t_bf[r]], t_block, [t_own[...]], [t_bf[r, rows_of(t_block), :]]
            )
            t_new = t_own[...] * total[:, :FRM] / (denom_t + epsilon)
            t_own[...] = t_new
            t_bf[r + 1, rows_of(t_block), :] = t_new.astype(BF16)
            mine = t_bf.at[r + 1, rows_of(t_block)]
            for dx, dzh, dc in PIX_STEPS:
                sem = at + (FAR if dzh else NEAR)
                remote(mine, mine, sem, pix_device(*pix_at(dx, dzh, dc))).start()
            remote(t_own, t_across, at + ACROSS, (p, frm_at(2, 0))).start()
            for part, sem, count in ((0, NEAR, CHIPS - 1), (1, FAR, CHIPS)):
                wait_bytes(t_bf.at[r + 1, pl.ds(0, count * ROWS)], recv_sem.at[at + sem])
                if part:
                    make_gram(r + 1)
                    send_gram(r + 1)
                group = lax.rem(zh + part, 2)
                spans = [pl.ds(pl.multiple_of(b * HALF + group * 64, 64), 64) for b in range(2)]
                t_rows = jnp.concatenate([t_bf[r + 1, span, :] for span in spans], axis=0)
                first = lax.rem(zl + group, 2)
                for h in range(SPLIT):
                    rows = dot_nn(t_rows, norm_t[h]).astype(BF16)
                    for b, span in enumerate(spans):
                        numer_part[r + 1, h, span, :] = rows[b * 64 : (b + 1) * 64]
                for h in range(SPLIT):
                    for i in (2, 0):
                        for dy in (2, 1, 3, 0):
                            other = frm_at(first + i, dy)
                            if i or dy:
                                send_numer(r + 1, h, [other])
                            else:

                                @pl.when(first > 0)
                                def _():
                                    send_numer(r + 1, h, [other])

            for h in range(SPLIT):
                numer_in[r + 1, h, f] = numer_part[r + 1, h, rows_of(f), :]
            t_turned[...] = t_bf[r + 1].T
        else:
            wait_bytes(t_across, recv_sem.at[at - PHASES + ACROSS])
            wait_bytes(chip_in.at[r], recv_sem.at[at + CHIP])
            total = summed(chip_in.at[r], CHIPS)
            t_across[...] = t_across[...] * total[:, :FRM] / (total[:, FRM:] + epsilon)
            for _, ozh, target in ends:
                place = t_out.at[rows_of(t_block)]

                @pl.when(ozh == zh)
                def _():
                    remote(t_across, place, at + NEAR, target).start()

                @pl.when(ozh != zh)
                def _():
                    remote(t_across, place, at + FAR, target).start()

            wait_bytes(s_low.at[pl.ds(0, 3)], recv_sem.at[at + LOW + 1])
            for h in range(SPLIT):
                pixels = pl.ds(h * PART, PART)
                low = jnp.concatenate(
                    [s_low[block % 4, block // 4, :, pixels] for block in range(GROUP)], axis=0
                )
                s_out[pixels, :] = (s_bf[r + 1, h].astype(F32) + low.astype(F32)).T
            for part, sem, count in ((0, NEAR, 4), (1, FAR, 4)):
                wait_bytes(t_out.at[pl.ds(0, count * ROWS)], recv_sem.at[at + sem])
                group = lax.rem(zh + part, 2)
                got = t_out.at[pl.ds(pl.multiple_of(c * HALF + group * 64, 64), 64)]
                remote(got, got, at + RELAY + part, pix_device(x, zh, 1 - c)).start()
            for part in range(2):
                wait_bytes(t_out.at[pl.ds(0, 64)], recv_sem.at[at + RELAY + part])

    @pl.when(has_right)
    def _():
        for copy in halos[0::2]:
            copy.wait_send()

    @pl.when(has_left)
    def _():
        for copy in halos[1::2]:
            copy.wait_send()

    for r in range(ROUNDS):
        last = r == ROUNDS - 1
        at = r * PHASES
        sent = [
            (GRAM, gram_in.at[r, pl.ds(0, GROUP - 1)]),
            (CORE_GRAM, gram_own.at[r, :, pl.ds(0, HALF)]),
            (CORE, core_in.at[r]),
            (CHIP, chip_in.at[r, pl.ds(0, CHIPS if last else CHIPS - 1)]),
        ]
        for h in range(SPLIT):
            sent.append((NUMER + h, numer_in.at[r, h, pl.ds(0, GROUP - 1)]))
            sent.append((SHARE + h, s_bf.at[r + 1, h, pl.ds(0, COMP - ROWS)]))
        if last:
            sent += [(LOW, s_low.at[0, pl.ds(0, 3)]), (LOW + 1, s_low.at[pl.ds(0, 3)])]
            sent += [(sem, t_out.at[pl.ds(0, 4 * ROWS)]) for sem in (NEAR, FAR)]
            sent += [(RELAY + part, t_out.at[pl.ds(0, 64)]) for part in range(2)]
        else:
            sent += [
                (NEAR, t_bf.at[r + 1, pl.ds(0, 7 * ROWS)]),
                (FAR, t_bf.at[r + 1, pl.ds(0, 8 * ROWS)]),
                (ACROSS, t_across),
            ]
        for sem, ref in sent:
            wait_bytes(ref, send_sem.at[at + sem])


def hand_on(s_v, t_v, s_out, t_out, sem):
    copies = [
        pltpu.make_async_copy(s_v, s_out, sem.at[0]),
        pltpu.make_async_copy(t_v, t_out, sem.at[1]),
    ]
    for copy in copies:
        copy.start()
    for copy in copies:
        copy.wait()


def on_device(movie, taps, scale, base, spatial, temporal):
    hbm = pl.BlockSpec(memory_space=pltpu.HBM)
    vmem = pl.BlockSpec(memory_space=pltpu.VMEM)
    shapes = (
        jax.ShapeDtypeStruct((PIX, COMP), F32),
        jax.ShapeDtypeStruct((COMP, FRM), F32),
    )
    operands = [
        pltpu.with_memory_space_constraint(array, pltpu.HBM)
        for array in (movie, taps, scale, base, spatial, temporal)
    ]
    s, t = pl.pallas_call(
        kernel,
        out_shape=shapes,
        in_specs=[hbm] * 6,
        out_specs=(vmem, vmem),
        scratch_shapes=[
            pltpu.VMEM((PIX, 2 * FRM), BF16),
            pltpu.VMEM((TAPS,), F32),
            pltpu.VMEM((PIX,), F32),
            pltpu.VMEM((PIX,), F32),
            pltpu.VMEM((PIX, COMP), F32),
            pltpu.VMEM((COMP, FRM), F32),
            pltpu.VMEM((1, 2 * FRM), F32),
            pltpu.VMEM((SPLIT, FRM, PART), BF16),
            pltpu.VMEM((SPLIT, COMP, PART), F32),
            pltpu.VMEM((SPLIT, ROWS, PART), F32),
            pltpu.VMEM((ROWS, FRM), F32),
            pltpu.VMEM((ROWS, FRM), F32),
            pltpu.VMEM((ROUNDS, COMP, FRM), BF16),
            pltpu.VMEM((FRM, COMP), BF16),
            pltpu.VMEM((ROUNDS, COMP, HALF), BF16),
            pltpu.VMEM((ROUNDS, GROUP, ROWS, HALF), BF16),
            pltpu.VMEM((ROUNDS, ROWS, COMP), F32),
            pltpu.VMEM((ROUNDS, SPLIT, COMP, PART), BF16),
            pltpu.VMEM((ROUNDS, SPLIT, GROUP, ROWS, PART), BF16),
            pltpu.VMEM((ROUNDS + 1, SPLIT, COMP, PART), BF16),
            pltpu.VMEM((4, 4, ROWS, PIX), BF16),
            pltpu.VMEM((ROUNDS, COMP, FRM + COMP), BF16),
            pltpu.VMEM((ROUNDS, HALF, FRM + COMP), BF16),
            pltpu.VMEM((ROUNDS, HALF, FRM + COMP), BF16),
            pltpu.VMEM((ROUNDS, CHIPS, ROWS, FRM + COMP), BF16),
            pltpu.SemaphoreType.DMA((6,)),
            pltpu.SemaphoreType.DMA((2 * SPLIT,)),
            pltpu.SemaphoreType.DMA((2 * SPLIT,)),
            pltpu.SemaphoreType.DMA((ROUNDS * PHASES,)),
            pltpu.SemaphoreType.DMA((ROUNDS * PHASES,)),
            pltpu.SemaphoreType.REGULAR((4,)),
        ],
        compiler_params=pltpu.CompilerParams(
            collective_id=0, has_side_effects=True, vmem_limit_bytes=40 << 20
        ),
    )(*operands)
    return pl.pallas_call(
        hand_on,
        out_shape=shapes,
        in_specs=[vmem, vmem],
        out_specs=(hbm, hbm),
        scratch_shapes=[pltpu.SemaphoreType.DMA((2,))],
        compiler_params=pltpu.CompilerParams(vmem_limit_bytes=40 << 20),
    )(s, t)


def solution(mesh):
    placed = (P("pix", "frm"), P(), P("pix"), P("pix"), P("pix", None), P(None, "frm"))
    return jax.shard_map(
        on_device,
        mesh=mesh,
        in_specs=placed,
        out_specs=(P("pix", None), P(None, "frm")),
        check_vma=False,
    )
```

```python
import functools

import jax
import jax.numpy as jnp
from jax import lax
from jax.experimental import pallas as pl
from jax.experimental.pallas import tpu as pltpu
from jax.sharding import PartitionSpec as P

ROUNDS = 2
MESH = pl.DeviceIdType.MESH
F32 = jnp.float32
BF16 = jnp.bfloat16
epsilon = 1e-06

GROUP = 16
CHIPS = 8
PIX = 512
FRM = 256
COMP = 256
ROWS = COMP // GROUP
HALO = 128
SPLIT = 1
PART = PIX // SPLIT
HALF = COMP // 2
TAPS = 257


def far_first(steps, hops):
    return sorted(steps, key=lambda step: -hops(*step))


FRM_STEPS = far_first(
    [(dzl, dy) for dzl in range(4) for dy in range(4) if dzl or dy],
    lambda dzl, dy: dzl + min(dy, 4 - dy),
)
CHIP_STEPS = far_first(
    [(dx, dzh) for dx in range(4) for dzh in range(2) if dx or dzh],
    lambda dx, dzh: min(dx, 4 - dx) + 4 * dzh,
)
PIX_STEPS = far_first(
    [(dx, dzh, dc) for dx in range(4) for dzh in range(2) for dc in range(2) if dx or dzh or dc],
    lambda dx, dzh, dc: min(dx, 4 - dx) + 4 * dzh + 0.5 * dc,
)


def dot_nn(a, b):
    return lax.dot_general(a, b, (((1,), (0,)), ((), ())), preferred_element_type=F32)


def dot_nt(a, b):
    return lax.dot_general(a, b, (((1,), (1,)), ((), ())), preferred_element_type=F32)


def split(value):
    high = value.astype(BF16)
    return high, (value - high.astype(F32)).astype(BF16)


def product(gram, wholes, block, owns, own_copies):
    terms = jnp.concatenate(split(gram), axis=0)
    row = lax.broadcasted_iota(jnp.int32, gram.shape, 0)
    column = lax.broadcasted_iota(jnp.int32, gram.shape, 1)
    diagonal = jnp.sum(jnp.where(column == row + block * ROWS, gram, 0.0), axis=1, keepdims=True)
    results = []
    for whole, own, copy in zip(wholes, owns, own_copies):
        both = dot_nn(terms, whole)
        results.append(both[:ROWS] + both[ROWS:] + diagonal * (own - copy.astype(F32)))
    return results


def rows_of(index, count=ROWS):
    return pl.ds(pl.multiple_of(index * count, count), count)


def wait_bytes(ref, sem):
    pltpu.make_async_copy(ref, ref, sem).wait()


def summed(inbox, count):
    total = inbox[0].astype(F32)
    for slot in range(1, count):
        total = total + inbox[slot].astype(F32)
    return total


NUMER, GRAM, SHARE, LOW, CORE_GRAM, CORE, CHIP, NEAR, FAR, RELAY = 0, 2, 3, 5, 7, 8, 9, 10, 11, 12
ACROSS = 14
PHASES = 15


def kernel(
    movie_hbm, taps_hbm, scale_hbm, base_hbm, spatial_hbm, temporal_hbm,
    s_out, t_out,
    padded, taps_v, scale_v, base_v, spatial_v, temporal_v,
    coef, norm_t, s_zero_t, s_own, t_own, t_across, t_bf, t_turned,
    gram_part, gram_in, gram_own, numer_part, numer_in, s_bf, s_low,
    mixed_part, core_in, chip_part, chip_in,
    load_sem, halo_send, halo_recv, send_sem, recv_sem, met,
):
    p = lax.axis_index("pix")
    f = lax.axis_index("frm")
    x, zh, c = lax.div(p, 4), lax.rem(lax.div(p, 2), 2), lax.rem(p, 2)
    zl, y = lax.div(f, 4), lax.rem(f, 4)
    pix_block = zh * 4 + x
    t_block = c * CHIPS + pix_block

    def pix_at(dx, dzh, dc):
        return lax.rem(x + dx, 4), lax.rem(zh + dzh, 2), lax.rem(c + dc, 2)

    def pix_device(ox, ozh, oc):
        return ((ox * 2 + ozh) * 2 + oc, f)

    def frm_at(dzl, dy):
        return lax.rem(zl + dzl, 4) * 4 + lax.rem(y + dy, 4)

    barrier = pltpu.get_barrier_semaphore()
    x_line = [pix_device(*pix_at(dx, 0, 0)) for dx in (2, 1, 3)]
    partner = pix_device(x, zh, 1 - c)
    z_two = [(pix_device(x, 1 - zh, c)[0], frm_at(2, 0)), (p, frm_at(2, 0))]
    z_line = [(p, frm_at(dzl, 0)) for dzl in (3, 2, 1)]
    y_line = [(p, frm_at(0, dy)) for dy in (2, 1, 3)]

    def signal(sem, targets):
        for target in targets:
            pl.semaphore_signal(sem, inc=1, device_id=target, device_id_type=MESH)

    greeted = [*z_line, z_two[0], *x_line, *y_line, partner]
    signal(barrier, greeted)
    corner_right = jnp.logical_and(y == 3, f < GROUP - 1)
    corner_left = jnp.logical_and(y == 0, f > 0)

    @pl.when(corner_right)
    def _():
        signal(barrier, [(p, f + 1)])

    @pl.when(corner_left)
    def _():
        signal(barrier, [(p, f - 1)])

    loads = [
        pltpu.make_async_copy(src, dst, load_sem.at[i])
        for i, (src, dst) in enumerate(
            (
                (movie_hbm, padded.at[:, pl.ds(HALO, FRM)]),
                (temporal_hbm, temporal_v),
                (spatial_hbm, spatial_v),
                (taps_hbm, taps_v),
                (scale_hbm, scale_v),
                (base_hbm, base_v),
            )
        )
    ]
    for copy in loads:
        copy.start()

    def remote(src, dst, sem, target):
        return pltpu.make_async_remote_copy(
            src_ref=src,
            dst_ref=dst,
            send_sem=send_sem.at[sem],
            recv_sem=recv_sem.at[sem],
            device_id=target,
            device_id_type=MESH,
        )

    cornered = jnp.logical_or(corner_right, corner_left)

    @pl.when(cornered)
    def _():
        pl.semaphore_wait(barrier, len(greeted) + 1)

    @pl.when(jnp.logical_not(cornered))
    def _():
        pl.semaphore_wait(barrier, len(greeted))

    met_frm, met_two, met_line, met_pix = (met.at[i] for i in range(4))
    loads[0].wait()
    halos = []
    for h in range(SPLIT):
        pixels = pl.ds(h * PART, PART)
        for side, (source, target, step) in enumerate(
            ((FRM, 0, 1), (HALO, HALO + FRM, GROUP - 1))
        ):
            halos.append(
                pltpu.make_async_remote_copy(
                    src_ref=padded.at[pixels, pl.ds(source, HALO)],
                    dst_ref=padded.at[pixels, pl.ds(target, HALO)],
                    send_sem=halo_send.at[2 * h + side],
                    recv_sem=halo_recv.at[2 * h + side],
                    device_id=(p, lax.rem(f + step, GROUP)),
                    device_id_type=MESH,
                )
            )
    has_right, has_left = f < GROUP - 1, f > 0

    @pl.when(has_right)
    def _():
        for copy in halos[0::2]:
            copy.start()

    @pl.when(has_left)
    def _():
        for copy in halos[1::2]:
            copy.start()

    signal(met_frm, z_line)
    signal(met_two, [*z_two, *x_line, partner])

    def make_gram(r):
        t_now = t_bf[r]
        t_half = t_bf[r, rows_of(c, HALF), :]
        gram_part[r] = dot_nt(t_now, t_half).astype(BF16)

    def send_gram(r):
        for dzl, dy in FRM_STEPS:
            other = frm_at(dzl, dy)
            remote(
                gram_part.at[r, rows_of(other)], gram_in.at[r, f], r * PHASES + GRAM, (p, other)
            ).start()
        gram_in[r, f] = gram_part[r, rows_of(f), :]

    def finish_gram(r):
        wait_bytes(gram_in.at[r, pl.ds(0, GROUP - 1)], recv_sem.at[r * PHASES + GRAM])
        half = pl.ds(pl.multiple_of(c * HALF, HALF), HALF)
        gram_own[r, :, half] = summed(gram_in.at[r], GROUP)
        mine = gram_own.at[r, :, half]
        copy = remote(mine, mine, r * PHASES + CORE_GRAM, pix_device(x, zh, 1 - c))
        copy.start()
        copy.wait_recv()

    loads[1].wait()
    t_bf[0] = temporal_v[...].astype(BF16)
    make_gram(0)
    pl.semaphore_wait(met_frm, len(z_line))
    send_gram(0)

    @pl.when(f == 0)
    def _():
        padded[:, pl.ds(0, HALO)] = jnp.zeros((PIX, HALO), BF16)

    @pl.when(f == GROUP - 1)
    def _():
        padded[:, pl.ds(HALO + FRM, HALO)] = jnp.zeros((PIX, HALO), BF16)

    for copy in loads[2:]:
        copy.wait()
    coef[...] = jnp.zeros_like(coef)
    centre = lax.broadcasted_iota(jnp.int32, (1, TAPS), 1) == HALO
    coef[:, pl.ds(0, TAPS)] = jnp.where(centre, 1.0, 0.0).astype(F32) - taps_v[...][None]
    band_t = pltpu.roll(
        jnp.broadcast_to(coef[...], (FRM, 2 * FRM)), 0, 1, stride=1, stride_axis=0
    ).astype(BF16)
    spatial_t = spatial_v[...].T
    for h in range(SPLIT):
        s_zero_t[h] = spatial_t[:, h * PART : (h + 1) * PART]
        s_bf[0, h] = s_zero_t[h].astype(BF16)
        s_own[h] = s_zero_t[h, rows_of(f), :]
    t_own[...] = temporal_v[rows_of(t_block), :]
    pl.semaphore_wait(met_two, len(z_two) + len(x_line) + 1)
    signal(met_line, [*x_line, partner])

    def send_numer(r, h, others):
        for other in others:
            remote(
                numer_part.at[r, h, rows_of(other)],
                numer_in.at[r, h, f],
                r * PHASES + NUMER + h,
                (p, other),
            ).start()

    for h in range(SPLIT):
        pixels = pl.ds(h * PART, PART)

        @pl.when(has_left)
        def _():
            halos[2 * h].wait_recv()

        @pl.when(has_right)
        def _():
            halos[2 * h + 1].wait_recv()

        mixed = dot_nt(band_t, padded[pixels, :])
        scaled = scale_v[pixels][None] * mixed + base_v[pixels][None]
        norm_t[h] = jnp.maximum(scaled, 0.0).astype(BF16)
        numer_part[0, h] = dot_nn(t_bf[0], norm_t[h]).astype(BF16)
        send_numer(0, h, [frm_at(dzl, dy) for dzl, dy in FRM_STEPS])
        numer_in[0, h, f] = numer_part[0, h, rows_of(f), :]

    chips, ends = [], []
    for dx, dzh in CHIP_STEPS:
        ox, ozh, _ = pix_at(dx, dzh, 0)
        chips.append((ox, ozh, pix_device(ox, ozh, c)))
    for dx in (2, 1, 3, 0):
        for ozh in range(2):
            ox = lax.rem(x + dx, 4)
            ends.append((ox, ozh, ((ox * 2 + ozh) * 2 + c, frm_at(2, 0))))

    pl.semaphore_wait(met_line, len(x_line) + 1)
    signal(met_pix, [partner])

    def left(r, *names):
        last = r == ROUNDS - 1
        temporal_rows = t_out if last else t_bf.at[ROUNDS - 1]
        refs = {
            GRAM: gram_in.at[r, pl.ds(0, GROUP - 1)],
            CORE_GRAM: gram_own.at[r, :, pl.ds(0, HALF)],
            CORE: core_in.at[r],
            CHIP: chip_in.at[r, pl.ds(0, CHIPS if last else CHIPS - 1)],
            NEAR: temporal_rows.at[pl.ds(0, (4 if last else 7) * ROWS)],
            FAR: temporal_rows.at[pl.ds(0, (4 if last else 8) * ROWS)],
            LOW: s_low.at[0, pl.ds(0, 3)],
            LOW + 1: s_low.at[pl.ds(0, 3)],
            ACROSS: t_across,
            RELAY: t_out.at[pl.ds(0, 64)],
            RELAY + 1: t_out.at[pl.ds(0, 64)],
        }
        for h in range(SPLIT):
            refs[NUMER + h] = numer_in.at[r, h, pl.ds(0, GROUP - 1)]
            refs[SHARE + h] = s_bf.at[r + 1, h, pl.ds(0, COMP - ROWS)]
        for name in names:
            wait_bytes(refs[name], send_sem.at[r * PHASES + name])

    spatial_phases = [GRAM, CORE_GRAM, *(NUMER + h for h in range(SPLIT))]
    spatial_phases += [SHARE + h for h in range(SPLIT)]

    for r in range(ROUNDS):
        last = r == ROUNDS - 1
        at = r * PHASES
        finish_gram(r)
        denoms = product(
            gram_own[r],
            [s_bf[r, h] for h in range(SPLIT)],
            f,
            [s_own[h] for h in range(SPLIT)],
            [s_bf[r, h, rows_of(f), :] for h in range(SPLIT)],
        )
        for h in range(SPLIT):
            wait_bytes(numer_in.at[r, h, pl.ds(0, GROUP - 1)], recv_sem.at[at + NUMER + h])
            numer = summed(numer_in.at[r, h], GROUP)
            s_new = s_own[h] * numer / (denoms[h] + epsilon)
            s_own[h] = s_new
            high, low = split(s_new)
            s_bf[r + 1, h, rows_of(f), :] = high
            mine = s_bf.at[r + 1, h, rows_of(f)]
            for dzl, dy in FRM_STEPS:
                remote(mine, mine, at + SHARE + h, (p, frm_at(dzl, dy))).start()
            if last:
                s_low[y, zl, :, pl.ds(h * PART, PART)] = low

        if last:
            for target in z_line:
                remote(s_low.at[y, zl], s_low.at[y, zl], at + LOW, target).start()

        numer_t = second_t = 0.0
        for h in range(SPLIT):
            wait_bytes(s_bf.at[r + 1, h, pl.ds(0, COMP - ROWS)], recv_sem.at[at + SHARE + h])
            s_now = s_bf[r + 1, h]
            numer_t = numer_t + dot_nt(s_now, norm_t[h])
            if last:
                second = dot_nn(t_turned[...], s_now).astype(BF16)
            else:
                second = s_now
            second_t = second_t + dot_nt(s_now, second)
        mixed_part[r, :, pl.ds(0, FRM)] = numer_t.astype(BF16)
        mixed_part[r, :, pl.ds(FRM, COMP)] = second_t.astype(BF16)
        remote(
            mixed_part.at[r, rows_of(1 - c, HALF)],
            core_in.at[r],
            at + CORE,
            pix_device(x, zh, 1 - c),
        ).start()
        wait_bytes(core_in.at[r], recv_sem.at[at + CORE])
        chip_sum = mixed_part[r, rows_of(c, HALF), :].astype(F32) + core_in[r].astype(F32)
        chip_part[r] = chip_sum.astype(BF16)
        if not r:
            pl.semaphore_wait(met_pix, 1)
        for ox, ozh, target in ends if last else chips:
            remote(
                chip_part.at[r, rows_of(ozh * 4 + ox)],
                chip_in.at[r, pix_block],
                at + CHIP,
                target,
            ).start()
        if last:
            wait_bytes(s_low.at[0, pl.ds(0, 3)], recv_sem.at[at + LOW])
            for target in y_line:
                remote(s_low.at[y], s_low.at[y], at + LOW + 1, target).start()
        if not r:

            @pl.when(has_right)
            def _():
                for copy in halos[0::2]:
                    copy.wait_send()

            @pl.when(has_left)
            def _():
                for copy in halos[1::2]:
                    copy.wait_send()

        left(r, *spatial_phases, CORE)
        if not last:
            chip_in[r, pix_block] = chip_part[r, rows_of(pix_block), :]
            wait_bytes(chip_in.at[r, pl.ds(0, CHIPS - 1)], recv_sem.at[at + CHIP])
            total = summed(chip_in.at[r], CHIPS)
            (denom_t,) = product(
                total[:, FRM:], [t_bf[r]], t_block, [t_own[...]], [t_bf[r, rows_of(t_block), :]]
            )
            t_new = t_own[...] * total[:, :FRM] / (denom_t + epsilon)
            t_own[...] = t_new
            t_bf[r + 1, rows_of(t_block), :] = t_new.astype(BF16)
            mine = t_bf.at[r + 1, rows_of(t_block)]
            for dx, dzh, dc in PIX_STEPS:
                sem = at + (FAR if dzh else NEAR)
                remote(mine, mine, sem, pix_device(*pix_at(dx, dzh, dc))).start()
            remote(t_own, t_across, at + ACROSS, (p, frm_at(2, 0))).start()
            for part, sem, count in ((0, NEAR, CHIPS - 1), (1, FAR, CHIPS)):
                wait_bytes(t_bf.at[r + 1, pl.ds(0, count * ROWS)], recv_sem.at[at + sem])
                if part:
                    make_gram(r + 1)
                    send_gram(r + 1)
                group = lax.rem(zh + part, 2)
                spans = [pl.ds(pl.multiple_of(b * HALF + group * 64, 64), 64) for b in range(2)]
                t_rows = jnp.concatenate([t_bf[r + 1, span, :] for span in spans], axis=0)
                first = lax.rem(zl + group, 2)
                for h in range(SPLIT):
                    rows = dot_nn(t_rows, norm_t[h]).astype(BF16)
                    for b, span in enumerate(spans):
                        numer_part[r + 1, h, span, :] = rows[b * 64 : (b + 1) * 64]
                for h in range(SPLIT):
                    for i in (2, 0):
                        for dy in (2, 1, 3, 0):
                            other = frm_at(first + i, dy)
                            if i or dy:
                                send_numer(r + 1, h, [other])
                            else:

                                @pl.when(first > 0)
                                def _():
                                    send_numer(r + 1, h, [other])

            for h in range(SPLIT):
                numer_in[r + 1, h, f] = numer_part[r + 1, h, rows_of(f), :]
            t_turned[...] = t_bf[r + 1].T
        else:
            wait_bytes(t_across, recv_sem.at[at - PHASES + ACROSS])
            wait_bytes(chip_in.at[r], recv_sem.at[at + CHIP])
            total = summed(chip_in.at[r], CHIPS)
            t_across[...] = t_across[...] * total[:, :FRM] / (total[:, FRM:] + epsilon)
            for _, ozh, target in ends:
                place = t_out.at[rows_of(t_block)]

                @pl.when(ozh == zh)
                def _():
                    remote(t_across, place, at + NEAR, target).start()

                @pl.when(ozh != zh)
                def _():
                    remote(t_across, place, at + FAR, target).start()

            left(r - 1, CHIP, NEAR, FAR, ACROSS)
            left(r, CHIP, LOW, LOW + 1)
            wait_bytes(s_low.at[pl.ds(0, 3)], recv_sem.at[at + LOW + 1])
            for h in range(SPLIT):
                pixels = pl.ds(h * PART, PART)
                low = jnp.concatenate(
                    [s_low[block % 4, block // 4, :, pixels] for block in range(GROUP)], axis=0
                )
                s_out[pixels, :] = (s_bf[r + 1, h].astype(F32) + low.astype(F32)).T
            for part, sem, count in ((0, NEAR, 4), (1, FAR, 4)):
                wait_bytes(t_out.at[pl.ds(0, count * ROWS)], recv_sem.at[at + sem])
                group = lax.rem(zh + part, 2)
                got = t_out.at[pl.ds(pl.multiple_of(c * HALF + group * 64, 64), 64)]
                remote(got, got, at + RELAY + part, pix_device(x, zh, 1 - c)).start()
            for part in range(2):
                wait_bytes(t_out.at[pl.ds(0, 64)], recv_sem.at[at + RELAY + part])
            left(r, NEAR, FAR, RELAY, RELAY + 1)


def hand_on(s_v, t_v, s_out, t_out, sem):
    copies = [
        pltpu.make_async_copy(s_v, s_out, sem.at[0]),
        pltpu.make_async_copy(t_v, t_out, sem.at[1]),
    ]
    for copy in copies:
        copy.start()
    for copy in copies:
        copy.wait()


def on_device(movie, taps, scale, base, spatial, temporal):
    hbm = pl.BlockSpec(memory_space=pltpu.HBM)
    vmem = pl.BlockSpec(memory_space=pltpu.VMEM)
    shapes = (
        jax.ShapeDtypeStruct((PIX, COMP), F32),
        jax.ShapeDtypeStruct((COMP, FRM), F32),
    )
    operands = [
        pltpu.with_memory_space_constraint(array, pltpu.HBM)
        for array in (movie, taps, scale, base, spatial, temporal)
    ]
    s, t = pl.pallas_call(
        kernel,
        out_shape=shapes,
        in_specs=[hbm] * 6,
        out_specs=(vmem, vmem),
        scratch_shapes=[
            pltpu.VMEM((PIX, 2 * FRM), BF16),
            pltpu.VMEM((TAPS,), F32),
            pltpu.VMEM((PIX,), F32),
            pltpu.VMEM((PIX,), F32),
            pltpu.VMEM((PIX, COMP), F32),
            pltpu.VMEM((COMP, FRM), F32),
            pltpu.VMEM((1, 2 * FRM), F32),
            pltpu.VMEM((SPLIT, FRM, PART), BF16),
            pltpu.VMEM((SPLIT, COMP, PART), F32),
            pltpu.VMEM((SPLIT, ROWS, PART), F32),
            pltpu.VMEM((ROWS, FRM), F32),
            pltpu.VMEM((ROWS, FRM), F32),
            pltpu.VMEM((ROUNDS, COMP, FRM), BF16),
            pltpu.VMEM((FRM, COMP), BF16),
            pltpu.VMEM((ROUNDS, COMP, HALF), BF16),
            pltpu.VMEM((ROUNDS, GROUP, ROWS, HALF), BF16),
            pltpu.VMEM((ROUNDS, ROWS, COMP), F32),
            pltpu.VMEM((ROUNDS, SPLIT, COMP, PART), BF16),
            pltpu.VMEM((ROUNDS, SPLIT, GROUP, ROWS, PART), BF16),
            pltpu.VMEM((ROUNDS + 1, SPLIT, COMP, PART), BF16),
            pltpu.VMEM((4, 4, ROWS, PIX), BF16),
            pltpu.VMEM((ROUNDS, COMP, FRM + COMP), BF16),
            pltpu.VMEM((ROUNDS, HALF, FRM + COMP), BF16),
            pltpu.VMEM((ROUNDS, HALF, FRM + COMP), BF16),
            pltpu.VMEM((ROUNDS, CHIPS, ROWS, FRM + COMP), BF16),
            pltpu.SemaphoreType.DMA((6,)),
            pltpu.SemaphoreType.DMA((2 * SPLIT,)),
            pltpu.SemaphoreType.DMA((2 * SPLIT,)),
            pltpu.SemaphoreType.DMA((ROUNDS * PHASES,)),
            pltpu.SemaphoreType.DMA((ROUNDS * PHASES,)),
            pltpu.SemaphoreType.REGULAR((4,)),
        ],
        compiler_params=pltpu.CompilerParams(
            collective_id=0, has_side_effects=True, vmem_limit_bytes=40 << 20
        ),
    )(*operands)
    return pl.pallas_call(
        hand_on,
        out_shape=shapes,
        in_specs=[vmem, vmem],
        out_specs=(hbm, hbm),
        scratch_shapes=[pltpu.SemaphoreType.DMA((2,))],
        compiler_params=pltpu.CompilerParams(vmem_limit_bytes=40 << 20),
    )(s, t)


def solution(mesh):
    placed = (P("pix", "frm"), P(), P("pix"), P("pix"), P("pix", None), P(None, "frm"))
    return jax.shard_map(
        on_device,
        mesh=mesh,
        in_specs=placed,
        out_specs=(P("pix", None), P(None, "frm")),
        check_vma=False,
    )
```

```python
import functools

import jax
import jax.numpy as jnp
from jax import lax
from jax.experimental import pallas as pl
from jax.experimental.pallas import tpu as pltpu
from jax.sharding import PartitionSpec as P

ROUNDS = 2
MESH = pl.DeviceIdType.MESH
F32 = jnp.float32
BF16 = jnp.bfloat16
epsilon = 1e-06

GROUP = 16
CHIPS = 8
PIX = 512
FRM = 256
COMP = 256
ROWS = COMP // GROUP
HALO = 128
SPLIT = 1
PART = PIX // SPLIT
HALF = COMP // 2
TAPS = 257


def far_first(steps, hops):
    return sorted(steps, key=lambda step: -hops(*step))


Y_STEPS = (2, 1, 3, 0)
CHIP_STEPS = far_first(
    [(dx, dzh) for dx in range(4) for dzh in range(2) if dx or dzh],
    lambda dx, dzh: min(dx, 4 - dx) + 4 * dzh,
)
PIX_STEPS = far_first(
    [(dx, dzh, dc) for dx in range(4) for dzh in range(2) for dc in range(2) if dx or dzh or dc],
    lambda dx, dzh, dc: min(dx, 4 - dx) + 4 * dzh + 0.5 * dc,
)


def dot_nn(a, b):
    return lax.dot_general(a, b, (((1,), (0,)), ((), ())), preferred_element_type=F32)


def dot_nt(a, b):
    return lax.dot_general(a, b, (((1,), (1,)), ((), ())), preferred_element_type=F32)


def split(value):
    high = value.astype(BF16)
    return high, (value - high.astype(F32)).astype(BF16)


def product(gram, wholes, block, owns, own_copies):
    terms = jnp.concatenate(split(gram), axis=0)
    row = lax.broadcasted_iota(jnp.int32, gram.shape, 0)
    column = lax.broadcasted_iota(jnp.int32, gram.shape, 1)
    diagonal = jnp.sum(jnp.where(column == row + block * ROWS, gram, 0.0), axis=1, keepdims=True)
    results = []
    for whole, own, copy in zip(wholes, owns, own_copies):
        both = dot_nn(terms, whole)
        results.append(both[:ROWS] + both[ROWS:] + diagonal * (own - copy.astype(F32)))
    return results


def rows_of(index, count=ROWS):
    return pl.ds(pl.multiple_of(index * count, count), count)


def wait_bytes(ref, sem):
    pltpu.make_async_copy(ref, ref, sem).wait()


def summed(inbox, count):
    total = inbox[0].astype(F32)
    for slot in range(1, count):
        total = total + inbox[slot].astype(F32)
    return total


NUMER, GRAM, SHARE, LOW, CORE_GRAM, CORE, CHIP, NEAR, FAR, RELAY = 0, 2, 3, 5, 7, 8, 9, 10, 11, 12
ACROSS = 14
PHASES = 15


def kernel(
    movie_hbm, taps_hbm, scale_hbm, base_hbm, spatial_hbm, temporal_hbm,
    s_out, t_out,
    padded, taps_v, scale_v, base_v, spatial_v, temporal_v,
    coef, norm_t, s_zero_t, s_own, t_own, t_across, t_bf, t_turned,
    gram_part, gram_in, gram_own, numer_part, numer_in, s_bf, s_low,
    mixed_part, core_in, chip_part, chip_in,
    load_sem, halo_send, halo_recv, send_sem, recv_sem, met,
):
    p = lax.axis_index("pix")
    f = lax.axis_index("frm")
    x, zh, c = lax.div(p, 4), lax.rem(lax.div(p, 2), 2), lax.rem(p, 2)
    zl, y = lax.div(f, 4), lax.rem(f, 4)
    pix_block = zh * 4 + x
    t_block = c * CHIPS + pix_block

    def pix_at(dx, dzh, dc):
        return lax.rem(x + dx, 4), lax.rem(zh + dzh, 2), lax.rem(c + dc, 2)

    def pix_device(ox, ozh, oc):
        return ((ox * 2 + ozh) * 2 + oc, f)

    def frm_at(dzl, dy):
        return lax.rem(zl + dzl, 4) * 4 + lax.rem(y + dy, 4)

    mirrored, across, beside = 3 - zl, lax.rem(zl + 2, 4), zl + 1 - 2 * lax.rem(zl, 2)

    def in_plane(plane, steps=Y_STEPS):
        return [plane * 4 + lax.rem(y + dy, 4) for dy in steps]

    planes = (mirrored, across, beside, zl)
    frm_others = [
        plane * 4 + lax.rem(y + dy, 4) for dy in Y_STEPS for plane in (planes if dy else planes[:3])
    ]

    barrier = pltpu.get_barrier_semaphore()
    x_line = [pix_device(*pix_at(dx, 0, 0)) for dx in (2, 1, 3)]
    partner = pix_device(x, zh, 1 - c)
    z_two = [(pix_device(x, 1 - zh, c)[0], frm_at(2, 0)), (p, frm_at(2, 0))]
    z_line = [(p, plane * 4 + y) for plane in (mirrored, across, beside)]
    y_line = [(p, frm_at(0, dy)) for dy in (2, 1, 3)]

    def signal(sem, targets):
        for target in targets:
            pl.semaphore_signal(sem, inc=1, device_id=target, device_id_type=MESH)

    greeted = [*z_line, z_two[0], *x_line, *y_line, partner]
    signal(barrier, greeted)
    corner_right = jnp.logical_and(y == 3, f < GROUP - 1)
    corner_left = jnp.logical_and(y == 0, f > 0)

    @pl.when(corner_right)
    def _():
        signal(barrier, [(p, f + 1)])

    @pl.when(corner_left)
    def _():
        signal(barrier, [(p, f - 1)])

    loads = [
        pltpu.make_async_copy(src, dst, load_sem.at[i])
        for i, (src, dst) in enumerate(
            (
                (movie_hbm, padded.at[:, pl.ds(HALO, FRM)]),
                (temporal_hbm, temporal_v),
                (spatial_hbm, spatial_v),
                (taps_hbm, taps_v),
                (scale_hbm, scale_v),
                (base_hbm, base_v),
            )
        )
    ]
    for copy in loads:
        copy.start()

    def remote(src, dst, sem, target):
        return pltpu.make_async_remote_copy(
            src_ref=src,
            dst_ref=dst,
            send_sem=send_sem.at[sem],
            recv_sem=recv_sem.at[sem],
            device_id=target,
            device_id_type=MESH,
        )

    cornered = jnp.logical_or(corner_right, corner_left)

    @pl.when(cornered)
    def _():
        pl.semaphore_wait(barrier, len(greeted) + 1)

    @pl.when(jnp.logical_not(cornered))
    def _():
        pl.semaphore_wait(barrier, len(greeted))

    met_frm, met_two, met_line, met_pix = (met.at[i] for i in range(4))
    loads[0].wait()
    halos = []
    for h in range(SPLIT):
        pixels = pl.ds(h * PART, PART)
        for side, (source, target, step) in enumerate(
            ((FRM, 0, 1), (HALO, HALO + FRM, GROUP - 1))
        ):
            halos.append(
                pltpu.make_async_remote_copy(
                    src_ref=padded.at[pixels, pl.ds(source, HALO)],
                    dst_ref=padded.at[pixels, pl.ds(target, HALO)],
                    send_sem=halo_send.at[2 * h + side],
                    recv_sem=halo_recv.at[2 * h + side],
                    device_id=(p, lax.rem(f + step, GROUP)),
                    device_id_type=MESH,
                )
            )
    has_right, has_left = f < GROUP - 1, f > 0

    @pl.when(has_right)
    def _():
        for copy in halos[0::2]:
            copy.start()

    @pl.when(has_left)
    def _():
        for copy in halos[1::2]:
            copy.start()

    signal(met_frm, z_line)
    signal(met_two, [*z_two, *x_line, partner])

    def make_gram(r):
        t_now = t_bf[r]
        t_half = t_bf[r, rows_of(c, HALF), :]
        gram_part[r] = dot_nt(t_now, t_half).astype(BF16)

    def send_gram(r):
        for other in frm_others:
            remote(
                gram_part.at[r, rows_of(other)], gram_in.at[r, f], r * PHASES + GRAM, (p, other)
            ).start()
        gram_in[r, f] = gram_part[r, rows_of(f), :]

    def finish_gram(r):
        wait_bytes(gram_in.at[r, pl.ds(0, GROUP - 1)], recv_sem.at[r * PHASES + GRAM])
        half = pl.ds(pl.multiple_of(c * HALF, HALF), HALF)
        gram_own[r, :, half] = summed(gram_in.at[r], GROUP)
        mine = gram_own.at[r, :, half]
        copy = remote(mine, mine, r * PHASES + CORE_GRAM, pix_device(x, zh, 1 - c))
        copy.start()
        copy.wait_recv()

    loads[1].wait()
    t_bf[0] = temporal_v[...].astype(BF16)
    make_gram(0)
    pl.semaphore_wait(met_frm, len(z_line))
    send_gram(0)

    @pl.when(f == 0)
    def _():
        padded[:, pl.ds(0, HALO)] = jnp.zeros((PIX, HALO), BF16)

    @pl.when(f == GROUP - 1)
    def _():
        padded[:, pl.ds(HALO + FRM, HALO)] = jnp.zeros((PIX, HALO), BF16)

    for copy in loads[2:]:
        copy.wait()
    coef[...] = jnp.zeros_like(coef)
    centre = lax.broadcasted_iota(jnp.int32, (1, TAPS), 1) == HALO
    coef[:, pl.ds(0, TAPS)] = jnp.where(centre, 1.0, 0.0).astype(F32) - taps_v[...][None]
    band_t = pltpu.roll(
        jnp.broadcast_to(coef[...], (FRM, 2 * FRM)), 0, 1, stride=1, stride_axis=0
    ).astype(BF16)
    spatial_t = spatial_v[...].T
    for h in range(SPLIT):
        s_zero_t[h] = spatial_t[:, h * PART : (h + 1) * PART]
        s_bf[0, h] = s_zero_t[h].astype(BF16)
        s_own[h] = s_zero_t[h, rows_of(f), :]
    t_own[...] = temporal_v[rows_of(t_block), :]
    pl.semaphore_wait(met_two, len(z_two) + len(x_line) + 1)
    signal(met_line, [*x_line, partner])

    def send_numer(r, h, others):
        for other in others:
            remote(
                numer_part.at[r, h, rows_of(other)],
                numer_in.at[r, h, f],
                r * PHASES + NUMER + h,
                (p, other),
            ).start()

    for h in range(SPLIT):
        pixels = pl.ds(h * PART, PART)

        @pl.when(has_left)
        def _():
            halos[2 * h].wait_recv()

        @pl.when(has_right)
        def _():
            halos[2 * h + 1].wait_recv()

        mixed = dot_nt(band_t, padded[pixels, :])
        scaled = scale_v[pixels][None] * mixed + base_v[pixels][None]
        norm_t[h] = jnp.maximum(scaled, 0.0).astype(BF16)
        numer_part[0, h] = dot_nn(t_bf[0], norm_t[h]).astype(BF16)
        send_numer(0, h, frm_others)
        numer_in[0, h, f] = numer_part[0, h, rows_of(f), :]

    chips, ends = [], []
    for dx, dzh in CHIP_STEPS:
        ox, ozh, _ = pix_at(dx, dzh, 0)
        chips.append((ox, ozh, pix_device(ox, ozh, c)))
    for dx in (2, 1, 3, 0):
        for ozh in range(2):
            ox = lax.rem(x + dx, 4)
            ends.append((ox, ozh, ((ox * 2 + ozh) * 2 + c, frm_at(2, 0))))

    pl.semaphore_wait(met_line, len(x_line) + 1)
    signal(met_pix, [partner])

    def left(r, *names):
        last = r == ROUNDS - 1
        temporal_rows = t_out if last else t_bf.at[ROUNDS - 1]
        refs = {
            GRAM: gram_in.at[r, pl.ds(0, GROUP - 1)],
            CORE_GRAM: gram_own.at[r, :, pl.ds(0, HALF)],
            CORE: core_in.at[r],
            CHIP: chip_in.at[r, pl.ds(0, CHIPS if last else CHIPS - 1)],
            NEAR: temporal_rows.at[pl.ds(0, (4 if last else 7) * ROWS)],
            FAR: temporal_rows.at[pl.ds(0, (4 if last else 8) * ROWS)],
            LOW: s_low.at[0, pl.ds(0, 3)],
            LOW + 1: s_low.at[pl.ds(0, 3)],
            ACROSS: t_across,
            RELAY: t_out.at[pl.ds(0, 64)],
            RELAY + 1: t_out.at[pl.ds(0, 64)],
        }
        for h in range(SPLIT):
            refs[NUMER + h] = numer_in.at[r, h, pl.ds(0, GROUP - 1)]
            refs[SHARE + h] = s_bf.at[r + 1, h, pl.ds(0, COMP - ROWS)]
        for name in names:
            wait_bytes(refs[name], send_sem.at[r * PHASES + name])

    spatial_phases = [GRAM, CORE_GRAM, *(NUMER + h for h in range(SPLIT))]
    spatial_phases += [SHARE + h for h in range(SPLIT)]

    for r in range(ROUNDS):
        last = r == ROUNDS - 1
        at = r * PHASES
        finish_gram(r)
        denoms = product(
            gram_own[r],
            [s_bf[r, h] for h in range(SPLIT)],
            f,
            [s_own[h] for h in range(SPLIT)],
            [s_bf[r, h, rows_of(f), :] for h in range(SPLIT)],
        )
        for h in range(SPLIT):
            wait_bytes(numer_in.at[r, h, pl.ds(0, GROUP - 1)], recv_sem.at[at + NUMER + h])
            numer = summed(numer_in.at[r, h], GROUP)
            s_new = s_own[h] * numer / (denoms[h] + epsilon)
            s_own[h] = s_new
            high, low = split(s_new)
            s_bf[r + 1, h, rows_of(f), :] = high
            mine = s_bf.at[r + 1, h, rows_of(f)]
            for other in frm_others:
                remote(mine, mine, at + SHARE + h, (p, other)).start()
            if last:
                s_low[y, zl, :, pl.ds(h * PART, PART)] = low

        if last:
            for target in z_line:
                remote(s_low.at[y, zl], s_low.at[y, zl], at + LOW, target).start()

        numer_t = second_t = 0.0
        for h in range(SPLIT):
            wait_bytes(s_bf.at[r + 1, h, pl.ds(0, COMP - ROWS)], recv_sem.at[at + SHARE + h])
            s_now = s_bf[r + 1, h]
            numer_t = numer_t + dot_nt(s_now, norm_t[h])
            if last:
                second = dot_nn(t_turned[...], s_now).astype(BF16)
            else:
                second = s_now
            second_t = second_t + dot_nt(s_now, second)
        mixed_part[r, :, pl.ds(0, FRM)] = numer_t.astype(BF16)
        mixed_part[r, :, pl.ds(FRM, COMP)] = second_t.astype(BF16)
        remote(
            mixed_part.at[r, rows_of(1 - c, HALF)],
            core_in.at[r],
            at + CORE,
            pix_device(x, zh, 1 - c),
        ).start()
        wait_bytes(core_in.at[r], recv_sem.at[at + CORE])
        chip_sum = mixed_part[r, rows_of(c, HALF), :].astype(F32) + core_in[r].astype(F32)
        chip_part[r] = chip_sum.astype(BF16)
        if not r:
            pl.semaphore_wait(met_pix, 1)
        for ox, ozh, target in ends if last else chips:
            remote(
                chip_part.at[r, rows_of(ozh * 4 + ox)],
                chip_in.at[r, pix_block],
                at + CHIP,
                target,
            ).start()
        if last:
            wait_bytes(s_low.at[0, pl.ds(0, 3)], recv_sem.at[at + LOW])
            for target in y_line:
                remote(s_low.at[y], s_low.at[y], at + LOW + 1, target).start()
        if not r:

            @pl.when(has_right)
            def _():
                for copy in halos[0::2]:
                    copy.wait_send()

            @pl.when(has_left)
            def _():
                for copy in halos[1::2]:
                    copy.wait_send()

        left(r, *spatial_phases, CORE)
        if not last:
            chip_in[r, pix_block] = chip_part[r, rows_of(pix_block), :]
            wait_bytes(chip_in.at[r, pl.ds(0, CHIPS - 1)], recv_sem.at[at + CHIP])
            total = summed(chip_in.at[r], CHIPS)
            (denom_t,) = product(
                total[:, FRM:], [t_bf[r]], t_block, [t_own[...]], [t_bf[r, rows_of(t_block), :]]
            )
            t_new = t_own[...] * total[:, :FRM] / (denom_t + epsilon)
            t_own[...] = t_new
            t_bf[r + 1, rows_of(t_block), :] = t_new.astype(BF16)
            mine = t_bf.at[r + 1, rows_of(t_block)]
            for dx, dzh, dc in PIX_STEPS:
                sem = at + (FAR if dzh else NEAR)
                remote(mine, mine, sem, pix_device(*pix_at(dx, dzh, dc))).start()
            remote(t_own, t_across, at + ACROSS, (p, frm_at(2, 0))).start()
            for part, sem, count in ((0, NEAR, CHIPS - 1), (1, FAR, CHIPS)):
                wait_bytes(t_bf.at[r + 1, pl.ds(0, count * ROWS)], recv_sem.at[at + sem])
                if part:
                    make_gram(r + 1)
                    send_gram(r + 1)
                group = lax.rem(zh + part, 2)
                spans = [pl.ds(pl.multiple_of(b * HALF + group * 64, 64), 64) for b in range(2)]
                t_rows = jnp.concatenate([t_bf[r + 1, span, :] for span in spans], axis=0)
                odd = lax.rem(zl + group, 2)
                far_plane = across + odd * (mirrored - across)
                near_plane = zl + odd * (beside - zl)
                for h in range(SPLIT):
                    rows = dot_nn(t_rows, norm_t[h]).astype(BF16)
                    for b, span in enumerate(spans):
                        numer_part[r + 1, h, span, :] = rows[b * 64 : (b + 1) * 64]
                for h in range(SPLIT):
                    send_numer(r + 1, h, in_plane(far_plane) + in_plane(near_plane, Y_STEPS[:3]))

                    @pl.when(odd > 0)
                    def _():
                        send_numer(r + 1, h, in_plane(near_plane, Y_STEPS[3:]))

            for h in range(SPLIT):
                numer_in[r + 1, h, f] = numer_part[r + 1, h, rows_of(f), :]
            t_turned[...] = t_bf[r + 1].T
        else:
            wait_bytes(t_across, recv_sem.at[at - PHASES + ACROSS])
            wait_bytes(chip_in.at[r], recv_sem.at[at + CHIP])
            total = summed(chip_in.at[r], CHIPS)
            t_across[...] = t_across[...] * total[:, :FRM] / (total[:, FRM:] + epsilon)
            for _, ozh, target in ends:
                place = t_out.at[rows_of(t_block)]

                @pl.when(ozh == zh)
                def _():
                    remote(t_across, place, at + NEAR, target).start()

                @pl.when(ozh != zh)
                def _():
                    remote(t_across, place, at + FAR, target).start()

            left(r - 1, CHIP, NEAR, FAR, ACROSS)
            left(r, CHIP, LOW, LOW + 1)
            wait_bytes(s_low.at[pl.ds(0, 3)], recv_sem.at[at + LOW + 1])
            for h in range(SPLIT):
                pixels = pl.ds(h * PART, PART)
                low = jnp.concatenate(
                    [s_low[block % 4, block // 4, :, pixels] for block in range(GROUP)], axis=0
                )
                s_out[pixels, :] = (s_bf[r + 1, h].astype(F32) + low.astype(F32)).T
            for part, sem, count in ((0, NEAR, 4), (1, FAR, 4)):
                wait_bytes(t_out.at[pl.ds(0, count * ROWS)], recv_sem.at[at + sem])
                group = lax.rem(zh + part, 2)
                got = t_out.at[pl.ds(pl.multiple_of(c * HALF + group * 64, 64), 64)]
                remote(got, got, at + RELAY + part, pix_device(x, zh, 1 - c)).start()
            for part in range(2):
                wait_bytes(t_out.at[pl.ds(0, 64)], recv_sem.at[at + RELAY + part])
            left(r, NEAR, FAR, RELAY, RELAY + 1)


def hand_on(s_v, t_v, s_out, t_out, sem):
    copies = [
        pltpu.make_async_copy(s_v, s_out, sem.at[0]),
        pltpu.make_async_copy(t_v, t_out, sem.at[1]),
    ]
    for copy in copies:
        copy.start()
    for copy in copies:
        copy.wait()


def on_device(movie, taps, scale, base, spatial, temporal):
    hbm = pl.BlockSpec(memory_space=pltpu.HBM)
    vmem = pl.BlockSpec(memory_space=pltpu.VMEM)
    shapes = (
        jax.ShapeDtypeStruct((PIX, COMP), F32),
        jax.ShapeDtypeStruct((COMP, FRM), F32),
    )
    operands = [
        pltpu.with_memory_space_constraint(array, pltpu.HBM)
        for array in (movie, taps, scale, base, spatial, temporal)
    ]
    s, t = pl.pallas_call(
        kernel,
        out_shape=shapes,
        in_specs=[hbm] * 6,
        out_specs=(vmem, vmem),
        scratch_shapes=[
            pltpu.VMEM((PIX, 2 * FRM), BF16),
            pltpu.VMEM((TAPS,), F32),
            pltpu.VMEM((PIX,), F32),
            pltpu.VMEM((PIX,), F32),
            pltpu.VMEM((PIX, COMP), F32),
            pltpu.VMEM((COMP, FRM), F32),
            pltpu.VMEM((1, 2 * FRM), F32),
            pltpu.VMEM((SPLIT, FRM, PART), BF16),
            pltpu.VMEM((SPLIT, COMP, PART), F32),
            pltpu.VMEM((SPLIT, ROWS, PART), F32),
            pltpu.VMEM((ROWS, FRM), F32),
            pltpu.VMEM((ROWS, FRM), F32),
            pltpu.VMEM((ROUNDS, COMP, FRM), BF16),
            pltpu.VMEM((FRM, COMP), BF16),
            pltpu.VMEM((ROUNDS, COMP, HALF), BF16),
            pltpu.VMEM((ROUNDS, GROUP, ROWS, HALF), BF16),
            pltpu.VMEM((ROUNDS, ROWS, COMP), F32),
            pltpu.VMEM((ROUNDS, SPLIT, COMP, PART), BF16),
            pltpu.VMEM((ROUNDS, SPLIT, GROUP, ROWS, PART), BF16),
            pltpu.VMEM((ROUNDS + 1, SPLIT, COMP, PART), BF16),
            pltpu.VMEM((4, 4, ROWS, PIX), BF16),
            pltpu.VMEM((ROUNDS, COMP, FRM + COMP), BF16),
            pltpu.VMEM((ROUNDS, HALF, FRM + COMP), BF16),
            pltpu.VMEM((ROUNDS, HALF, FRM + COMP), BF16),
            pltpu.VMEM((ROUNDS, CHIPS, ROWS, FRM + COMP), BF16),
            pltpu.SemaphoreType.DMA((6,)),
            pltpu.SemaphoreType.DMA((2 * SPLIT,)),
            pltpu.SemaphoreType.DMA((2 * SPLIT,)),
            pltpu.SemaphoreType.DMA((ROUNDS * PHASES,)),
            pltpu.SemaphoreType.DMA((ROUNDS * PHASES,)),
            pltpu.SemaphoreType.REGULAR((4,)),
        ],
        compiler_params=pltpu.CompilerParams(
            collective_id=0, has_side_effects=True, vmem_limit_bytes=40 << 20
        ),
    )(*operands)
    return pl.pallas_call(
        hand_on,
        out_shape=shapes,
        in_specs=[vmem, vmem],
        out_specs=(hbm, hbm),
        scratch_shapes=[pltpu.SemaphoreType.DMA((2,))],
        compiler_params=pltpu.CompilerParams(vmem_limit_bytes=40 << 20),
    )(s, t)


def solution(mesh):
    placed = (P("pix", "frm"), P(), P("pix"), P("pix"), P("pix", None), P(None, "frm"))
    return jax.shard_map(
        on_device,
        mesh=mesh,
        in_specs=placed,
        out_specs=(P("pix", None), P(None, "frm")),
        check_vma=False,
    )
```

```python
import functools

import jax
import jax.numpy as jnp
from jax import lax
from jax.experimental import pallas as pl
from jax.experimental.pallas import tpu as pltpu
from jax.sharding import PartitionSpec as P

ROUNDS = 2
MESH = pl.DeviceIdType.MESH
F32 = jnp.float32
BF16 = jnp.bfloat16
epsilon = 1e-06

GROUP = 16
CHIPS = 8
PIX = 512
FRM = 256
COMP = 256
ROWS = COMP // GROUP
HALO = 128
SPLIT = 1
PART = PIX // SPLIT
HALF = COMP // 2
TAPS = 257


def far_first(steps, hops):
    return sorted(steps, key=lambda step: -hops(*step))


Y_STEPS = (2, 1, 3, 0)
CHIP_STEPS = far_first(
    [(dx, dzh) for dx in range(4) for dzh in range(2) if dx or dzh],
    lambda dx, dzh: min(dx, 4 - dx) + 4 * dzh,
)
PIX_STEPS = far_first(
    [(dx, dzh, dc) for dx in range(4) for dzh in range(2) for dc in range(2) if dx or dzh or dc],
    lambda dx, dzh, dc: min(dx, 4 - dx) + 4 * dzh + 0.5 * dc,
)


def dot_nn(a, b):
    return lax.dot_general(a, b, (((1,), (0,)), ((), ())), preferred_element_type=F32)


def dot_nt(a, b):
    return lax.dot_general(a, b, (((1,), (1,)), ((), ())), preferred_element_type=F32)


def split(value):
    high = value.astype(BF16)
    return high, (value - high.astype(F32)).astype(BF16)


def product(gram, wholes, block, owns, own_copies):
    terms = jnp.concatenate(split(gram), axis=0)
    row = lax.broadcasted_iota(jnp.int32, gram.shape, 0)
    column = lax.broadcasted_iota(jnp.int32, gram.shape, 1)
    diagonal = jnp.sum(jnp.where(column == row + block * ROWS, gram, 0.0), axis=1, keepdims=True)
    results = []
    for whole, own, copy in zip(wholes, owns, own_copies):
        both = dot_nn(terms, whole)
        results.append(both[:ROWS] + both[ROWS:] + diagonal * (own - copy.astype(F32)))
    return results


def rows_of(index, count=ROWS):
    return pl.ds(pl.multiple_of(index * count, count), count)


def wait_bytes(ref, sem):
    pltpu.make_async_copy(ref, ref, sem).wait()


def summed(inbox, count):
    total = inbox[0].astype(F32)
    for slot in range(1, count):
        total = total + inbox[slot].astype(F32)
    return total


NUMER, GRAM, SHARE, LOW, CORE_GRAM, CORE, CHIP, NEAR, FAR, RELAY = 0, 2, 3, 5, 7, 8, 9, 10, 11, 12
ACROSS = 14
PHASES = 15


def kernel(
    movie_hbm, taps_hbm, scale_hbm, base_hbm, spatial_hbm, temporal_hbm,
    s_out, t_out,
    padded, taps_v, scale_v, base_v, spatial_v, temporal_v,
    coef, norm_t, s_zero_t, s_own, t_own, t_across, t_bf, t_turned,
    gram_part, gram_in, gram_own, numer_part, numer_in, s_bf, s_low,
    mixed_part, core_in, chip_part, chip_in,
    load_sem, halo_send, halo_recv, send_sem, recv_sem, met,
):
    p = lax.axis_index("pix")
    f = lax.axis_index("frm")
    x, zh, c = lax.div(p, 4), lax.rem(lax.div(p, 2), 2), lax.rem(p, 2)
    zl, y = lax.div(f, 4), lax.rem(f, 4)
    pix_block = zh * 4 + x
    t_block = c * CHIPS + pix_block

    def pix_at(dx, dzh, dc):
        return lax.rem(x + dx, 4), lax.rem(zh + dzh, 2), lax.rem(c + dc, 2)

    def pix_device(ox, ozh, oc):
        return ((ox * 2 + ozh) * 2 + oc, f)

    def frm_at(dzl, dy):
        return lax.rem(zl + dzl, 4) * 4 + lax.rem(y + dy, 4)

    mirrored, across, beside = 3 - zl, lax.rem(zl + 2, 4), zl + 1 - 2 * lax.rem(zl, 2)

    def in_plane(plane, steps=Y_STEPS):
        return [plane * 4 + lax.rem(y + dy, 4) for dy in steps]

    planes = (mirrored, across, beside, zl)
    frm_others = [
        plane * 4 + lax.rem(y + dy, 4) for dy in Y_STEPS for plane in (planes if dy else planes[:3])
    ]

    barrier = pltpu.get_barrier_semaphore()
    x_line = [pix_device(*pix_at(dx, 0, 0)) for dx in (2, 1, 3)]
    partner = pix_device(x, zh, 1 - c)
    z_two = [(pix_device(x, 1 - zh, c)[0], frm_at(2, 0)), (p, frm_at(2, 0))]
    z_line = [(p, plane * 4 + y) for plane in (mirrored, across, beside)]
    y_line = [(p, frm_at(0, dy)) for dy in (2, 1, 3)]

    def signal(sem, targets):
        for target in targets:
            pl.semaphore_signal(sem, inc=1, device_id=target, device_id_type=MESH)

    greeted = [*z_line, z_two[0], *x_line, *y_line, partner]
    signal(barrier, greeted)
    corner_right = jnp.logical_and(y == 3, f < GROUP - 1)
    corner_left = jnp.logical_and(y == 0, f > 0)

    @pl.when(corner_right)
    def _():
        signal(barrier, [(p, f + 1)])

    @pl.when(corner_left)
    def _():
        signal(barrier, [(p, f - 1)])

    loads = [
        pltpu.make_async_copy(src, dst, load_sem.at[i])
        for i, (src, dst) in enumerate(
            (
                (movie_hbm, padded.at[:, pl.ds(HALO, FRM)]),
                (temporal_hbm, temporal_v),
                (spatial_hbm, spatial_v),
                (taps_hbm, taps_v),
                (scale_hbm, scale_v),
                (base_hbm, base_v),
            )
        )
    ]
    for copy in loads:
        copy.start()

    def remote(src, dst, sem, target):
        return pltpu.make_async_remote_copy(
            src_ref=src,
            dst_ref=dst,
            send_sem=send_sem.at[sem],
            recv_sem=recv_sem.at[sem],
            device_id=target,
            device_id_type=MESH,
        )

    cornered = jnp.logical_or(corner_right, corner_left)

    @pl.when(cornered)
    def _():
        pl.semaphore_wait(barrier, len(greeted) + 1)

    @pl.when(jnp.logical_not(cornered))
    def _():
        pl.semaphore_wait(barrier, len(greeted))

    met_frm, met_two, met_line, met_pix = (met.at[i] for i in range(4))
    loads[0].wait()
    halos = []
    for h in range(SPLIT):
        pixels = pl.ds(h * PART, PART)
        for side, (source, target, step) in enumerate(
            ((FRM, 0, 1), (HALO, HALO + FRM, GROUP - 1))
        ):
            halos.append(
                pltpu.make_async_remote_copy(
                    src_ref=padded.at[pixels, pl.ds(source, HALO)],
                    dst_ref=padded.at[pixels, pl.ds(target, HALO)],
                    send_sem=halo_send.at[2 * h + side],
                    recv_sem=halo_recv.at[2 * h + side],
                    device_id=(p, lax.rem(f + step, GROUP)),
                    device_id_type=MESH,
                )
            )
    has_right, has_left = f < GROUP - 1, f > 0

    @pl.when(has_right)
    def _():
        for copy in halos[0::2]:
            copy.start()

    @pl.when(has_left)
    def _():
        for copy in halos[1::2]:
            copy.start()

    signal(met_frm, z_line)
    signal(met_two, [*z_two, *x_line, partner])

    def make_gram(r):
        t_now = t_bf[r]
        t_half = t_bf[r, rows_of(c, HALF), :]
        gram_part[r] = dot_nt(t_now, t_half).astype(BF16)

    def send_gram(r):
        for other in frm_others:
            remote(
                gram_part.at[r, rows_of(other)], gram_in.at[r, f], r * PHASES + GRAM, (p, other)
            ).start()
        gram_in[r, f] = gram_part[r, rows_of(f), :]

    def finish_gram(r):
        wait_bytes(gram_in.at[r, pl.ds(0, GROUP - 1)], recv_sem.at[r * PHASES + GRAM])
        half = pl.ds(pl.multiple_of(c * HALF, HALF), HALF)
        gram_own[r, :, half] = summed(gram_in.at[r], GROUP)
        mine = gram_own.at[r, :, half]
        copy = remote(mine, mine, r * PHASES + CORE_GRAM, pix_device(x, zh, 1 - c))
        copy.start()
        copy.wait_recv()

    loads[1].wait()
    t_bf[0] = temporal_v[...].astype(BF16)
    make_gram(0)
    pl.semaphore_wait(met_frm, len(z_line))
    send_gram(0)

    @pl.when(f == 0)
    def _():
        padded[:, pl.ds(0, HALO)] = jnp.zeros((PIX, HALO), BF16)

    @pl.when(f == GROUP - 1)
    def _():
        padded[:, pl.ds(HALO + FRM, HALO)] = jnp.zeros((PIX, HALO), BF16)

    for copy in loads[2:]:
        copy.wait()
    coef[...] = jnp.zeros_like(coef)
    centre = lax.broadcasted_iota(jnp.int32, (1, TAPS), 1) == HALO
    coef[:, pl.ds(0, TAPS)] = jnp.where(centre, 1.0, 0.0).astype(F32) - taps_v[...][None]
    band_t = pltpu.roll(
        jnp.broadcast_to(coef[...], (FRM, 2 * FRM)), 0, 1, stride=1, stride_axis=0
    ).astype(BF16)
    spatial_t = spatial_v[...].T
    for h in range(SPLIT):
        s_zero_t[h] = spatial_t[:, h * PART : (h + 1) * PART]
        s_bf[0, h] = s_zero_t[h].astype(BF16)
        s_own[h] = s_zero_t[h, rows_of(f), :]
    t_own[...] = temporal_v[rows_of(t_block), :]
    pl.semaphore_wait(met_two, len(z_two) + len(x_line) + 1)
    signal(met_line, [*x_line, partner])

    def send_numer(r, h, others):
        for other in others:
            remote(
                numer_part.at[r, h, rows_of(other)],
                numer_in.at[r, h, f],
                r * PHASES + NUMER + h,
                (p, other),
            ).start()

    for h in range(SPLIT):
        pixels = pl.ds(h * PART, PART)

        @pl.when(has_left)
        def _():
            halos[2 * h].wait_recv()

        @pl.when(has_right)
        def _():
            halos[2 * h + 1].wait_recv()

        mixed = dot_nt(band_t, padded[pixels, :])
        scaled = scale_v[pixels][None] * mixed + base_v[pixels][None]
        norm_t[h] = jnp.maximum(scaled, 0.0).astype(BF16)
        numer_part[0, h] = dot_nn(t_bf[0], norm_t[h]).astype(BF16)
        send_numer(0, h, frm_others)
        numer_in[0, h, f] = numer_part[0, h, rows_of(f), :]

    chips, ends = [], []
    for dx, dzh in CHIP_STEPS:
        ox, ozh, _ = pix_at(dx, dzh, 0)
        chips.append((ox, ozh, pix_device(ox, ozh, c)))
    for dx in (2, 1, 3, 0):
        for ozh in range(2):
            ox = lax.rem(x + dx, 4)
            ends.append((ox, ozh, ((ox * 2 + ozh) * 2 + c, frm_at(2, 0))))

    pl.semaphore_wait(met_line, len(x_line) + 1)
    signal(met_pix, [partner])

    def left(r, *names):
        last = r == ROUNDS - 1
        temporal_rows = t_out if last else t_bf.at[ROUNDS - 1]
        refs = {
            GRAM: gram_in.at[r, pl.ds(0, GROUP - 1)],
            CORE_GRAM: gram_own.at[r, :, pl.ds(0, HALF)],
            CORE: core_in.at[r],
            CHIP: chip_in.at[r, pl.ds(0, CHIPS if last else CHIPS - 1)],
            NEAR: temporal_rows.at[pl.ds(0, (4 if last else 7) * ROWS)],
            FAR: temporal_rows.at[pl.ds(0, (4 if last else 8) * ROWS)],
            LOW: s_low.at[0, pl.ds(0, 3)],
            LOW + 1: s_low.at[pl.ds(0, 3)],
            ACROSS: t_across,
            RELAY: t_out.at[pl.ds(0, 64)],
            RELAY + 1: t_out.at[pl.ds(0, 64)],
        }
        for h in range(SPLIT):
            refs[NUMER + h] = numer_in.at[r, h, pl.ds(0, GROUP - 1)]
            refs[SHARE + h] = s_bf.at[r + 1, h, pl.ds(0, COMP - ROWS)]
        for name in names:
            wait_bytes(refs[name], send_sem.at[r * PHASES + name])

    spatial_phases = [GRAM, CORE_GRAM, *(NUMER + h for h in range(SPLIT))]
    spatial_phases += [SHARE + h for h in range(SPLIT)]

    for r in range(ROUNDS):
        last = r == ROUNDS - 1
        at = r * PHASES
        finish_gram(r)
        denoms = product(
            gram_own[r],
            [s_bf[r, h] for h in range(SPLIT)],
            f,
            [s_own[h] for h in range(SPLIT)],
            [s_bf[r, h, rows_of(f), :] for h in range(SPLIT)],
        )
        for h in range(SPLIT):
            wait_bytes(numer_in.at[r, h, pl.ds(0, GROUP - 1)], recv_sem.at[at + NUMER + h])
            numer = summed(numer_in.at[r, h], GROUP)
            s_new = s_own[h] * numer / (denoms[h] + epsilon)
            s_own[h] = s_new
            high, low = split(s_new)
            s_bf[r + 1, h, rows_of(f), :] = high
            mine = s_bf.at[r + 1, h, rows_of(f)]
            for other in frm_others:
                remote(mine, mine, at + SHARE + h, (p, other)).start()
            if last:
                s_low[y, zl, :, pl.ds(h * PART, PART)] = low

        numer_t = second_t = 0.0
        for h in range(SPLIT):
            wait_bytes(s_bf.at[r + 1, h, pl.ds(0, COMP - ROWS)], recv_sem.at[at + SHARE + h])
            s_now = s_bf[r + 1, h]
            numer_t = numer_t + dot_nt(s_now, norm_t[h])
            if last:
                second = dot_nn(t_turned[...], s_now).astype(BF16)
            else:
                second = s_now
            second_t = second_t + dot_nt(s_now, second)
        mixed_part[r, :, pl.ds(0, FRM)] = numer_t.astype(BF16)
        mixed_part[r, :, pl.ds(FRM, COMP)] = second_t.astype(BF16)
        remote(
            mixed_part.at[r, rows_of(1 - c, HALF)],
            core_in.at[r],
            at + CORE,
            pix_device(x, zh, 1 - c),
        ).start()
        if last:
            for target in z_line:
                remote(s_low.at[y, zl], s_low.at[y, zl], at + LOW, target).start()
        wait_bytes(core_in.at[r], recv_sem.at[at + CORE])
        chip_sum = mixed_part[r, rows_of(c, HALF), :].astype(F32) + core_in[r].astype(F32)
        chip_part[r] = chip_sum.astype(BF16)
        if not r:
            pl.semaphore_wait(met_pix, 1)
        for ox, ozh, target in ends if last else chips:
            remote(
                chip_part.at[r, rows_of(ozh * 4 + ox)],
                chip_in.at[r, pix_block],
                at + CHIP,
                target,
            ).start()
        if last:
            wait_bytes(s_low.at[0, pl.ds(0, 3)], recv_sem.at[at + LOW])
            for target in y_line:
                remote(s_low.at[y], s_low.at[y], at + LOW + 1, target).start()
        if not r:

            @pl.when(has_right)
            def _():
                for copy in halos[0::2]:
                    copy.wait_send()

            @pl.when(has_left)
            def _():
                for copy in halos[1::2]:
                    copy.wait_send()

        left(r, *spatial_phases, CORE)
        if not last:
            chip_in[r, pix_block] = chip_part[r, rows_of(pix_block), :]
            wait_bytes(chip_in.at[r, pl.ds(0, CHIPS - 1)], recv_sem.at[at + CHIP])
            total = summed(chip_in.at[r], CHIPS)
            (denom_t,) = product(
                total[:, FRM:], [t_bf[r]], t_block, [t_own[...]], [t_bf[r, rows_of(t_block), :]]
            )
            t_new = t_own[...] * total[:, :FRM] / (denom_t + epsilon)
            t_own[...] = t_new
            t_bf[r + 1, rows_of(t_block), :] = t_new.astype(BF16)
            mine = t_bf.at[r + 1, rows_of(t_block)]
            for dx, dzh, dc in PIX_STEPS:
                sem = at + (FAR if dzh else NEAR)
                remote(mine, mine, sem, pix_device(*pix_at(dx, dzh, dc))).start()
            remote(t_own, t_across, at + ACROSS, (p, frm_at(2, 0))).start()
            for part, sem, count in ((0, NEAR, CHIPS - 1), (1, FAR, CHIPS)):
                wait_bytes(t_bf.at[r + 1, pl.ds(0, count * ROWS)], recv_sem.at[at + sem])
                if part:
                    make_gram(r + 1)
                    send_gram(r + 1)
                group = lax.rem(zh + part, 2)
                spans = [pl.ds(pl.multiple_of(b * HALF + group * 64, 64), 64) for b in range(2)]
                t_rows = jnp.concatenate([t_bf[r + 1, span, :] for span in spans], axis=0)
                odd = lax.rem(zl + group, 2)
                far_plane = across + odd * (mirrored - across)
                near_plane = zl + odd * (beside - zl)
                for h in range(SPLIT):
                    rows = dot_nn(t_rows, norm_t[h]).astype(BF16)
                    for b, span in enumerate(spans):
                        numer_part[r + 1, h, span, :] = rows[b * 64 : (b + 1) * 64]
                for h in range(SPLIT):
                    send_numer(r + 1, h, in_plane(far_plane) + in_plane(near_plane, Y_STEPS[:3]))

                    @pl.when(odd > 0)
                    def _():
                        send_numer(r + 1, h, in_plane(near_plane, Y_STEPS[3:]))

            for h in range(SPLIT):
                numer_in[r + 1, h, f] = numer_part[r + 1, h, rows_of(f), :]
            t_turned[...] = t_bf[r + 1].T
        else:
            wait_bytes(t_across, recv_sem.at[at - PHASES + ACROSS])
            wait_bytes(chip_in.at[r], recv_sem.at[at + CHIP])
            total = summed(chip_in.at[r], CHIPS)
            t_across[...] = t_across[...] * total[:, :FRM] / (total[:, FRM:] + epsilon)
            for _, ozh, target in ends:
                place = t_out.at[rows_of(t_block)]

                @pl.when(ozh == zh)
                def _():
                    remote(t_across, place, at + NEAR, target).start()

                @pl.when(ozh != zh)
                def _():
                    remote(t_across, place, at + FAR, target).start()

            for part, sem, count in ((0, NEAR, 4), (1, FAR, 4)):
                wait_bytes(t_out.at[pl.ds(0, count * ROWS)], recv_sem.at[at + sem])
                group = lax.rem(zh + part, 2)
                got = t_out.at[pl.ds(pl.multiple_of(c * HALF + group * 64, 64), 64)]
                remote(got, got, at + RELAY + part, pix_device(x, zh, 1 - c)).start()
            left(r - 1, CHIP, NEAR, FAR, ACROSS)
            left(r, CHIP, LOW, LOW + 1)
            wait_bytes(s_low.at[pl.ds(0, 3)], recv_sem.at[at + LOW + 1])
            for h in range(SPLIT):
                pixels = pl.ds(h * PART, PART)
                low = jnp.concatenate(
                    [s_low[block % 4, block // 4, :, pixels] for block in range(GROUP)], axis=0
                )
                s_out[pixels, :] = (s_bf[r + 1, h].astype(F32) + low.astype(F32)).T
            for part in range(2):
                wait_bytes(t_out.at[pl.ds(0, 64)], recv_sem.at[at + RELAY + part])
            left(r, NEAR, FAR, RELAY, RELAY + 1)


def hand_on(s_v, t_v, s_out, t_out, sem):
    copies = [
        pltpu.make_async_copy(s_v, s_out, sem.at[0]),
        pltpu.make_async_copy(t_v, t_out, sem.at[1]),
    ]
    for copy in copies:
        copy.start()
    for copy in copies:
        copy.wait()


def on_device(movie, taps, scale, base, spatial, temporal):
    hbm = pl.BlockSpec(memory_space=pltpu.HBM)
    vmem = pl.BlockSpec(memory_space=pltpu.VMEM)
    shapes = (
        jax.ShapeDtypeStruct((PIX, COMP), F32),
        jax.ShapeDtypeStruct((COMP, FRM), F32),
    )
    operands = [
        pltpu.with_memory_space_constraint(array, pltpu.HBM)
        for array in (movie, taps, scale, base, spatial, temporal)
    ]
    s, t = pl.pallas_call(
        kernel,
        out_shape=shapes,
        in_specs=[hbm] * 6,
        out_specs=(vmem, vmem),
        scratch_shapes=[
            pltpu.VMEM((PIX, 2 * FRM), BF16),
            pltpu.VMEM((TAPS,), F32),
            pltpu.VMEM((PIX,), F32),
            pltpu.VMEM((PIX,), F32),
            pltpu.VMEM((PIX, COMP), F32),
            pltpu.VMEM((COMP, FRM), F32),
            pltpu.VMEM((1, 2 * FRM), F32),
            pltpu.VMEM((SPLIT, FRM, PART), BF16),
            pltpu.VMEM((SPLIT, COMP, PART), F32),
            pltpu.VMEM((SPLIT, ROWS, PART), F32),
            pltpu.VMEM((ROWS, FRM), F32),
            pltpu.VMEM((ROWS, FRM), F32),
            pltpu.VMEM((ROUNDS, COMP, FRM), BF16),
            pltpu.VMEM((FRM, COMP), BF16),
            pltpu.VMEM((ROUNDS, COMP, HALF), BF16),
            pltpu.VMEM((ROUNDS, GROUP, ROWS, HALF), BF16),
            pltpu.VMEM((ROUNDS, ROWS, COMP), F32),
            pltpu.VMEM((ROUNDS, SPLIT, COMP, PART), BF16),
            pltpu.VMEM((ROUNDS, SPLIT, GROUP, ROWS, PART), BF16),
            pltpu.VMEM((ROUNDS + 1, SPLIT, COMP, PART), BF16),
            pltpu.VMEM((4, 4, ROWS, PIX), BF16),
            pltpu.VMEM((ROUNDS, COMP, FRM + COMP), BF16),
            pltpu.VMEM((ROUNDS, HALF, FRM + COMP), BF16),
            pltpu.VMEM((ROUNDS, HALF, FRM + COMP), BF16),
            pltpu.VMEM((ROUNDS, CHIPS, ROWS, FRM + COMP), BF16),
            pltpu.SemaphoreType.DMA((6,)),
            pltpu.SemaphoreType.DMA((2 * SPLIT,)),
            pltpu.SemaphoreType.DMA((2 * SPLIT,)),
            pltpu.SemaphoreType.DMA((ROUNDS * PHASES,)),
            pltpu.SemaphoreType.DMA((ROUNDS * PHASES,)),
            pltpu.SemaphoreType.REGULAR((4,)),
        ],
        compiler_params=pltpu.CompilerParams(
            collective_id=0, has_side_effects=True, vmem_limit_bytes=40 << 20
        ),
    )(*operands)
    return pl.pallas_call(
        hand_on,
        out_shape=shapes,
        in_specs=[vmem, vmem],
        out_specs=(hbm, hbm),
        scratch_shapes=[pltpu.SemaphoreType.DMA((2,))],
        compiler_params=pltpu.CompilerParams(vmem_limit_bytes=40 << 20),
    )(s, t)


def solution(mesh):
    placed = (P("pix", "frm"), P(), P("pix"), P("pix"), P("pix", None), P(None, "frm"))
    return jax.shard_map(
        on_device,
        mesh=mesh,
        in_specs=placed,
        out_specs=(P("pix", None), P(None, "frm")),
        check_vma=False,
    )
```

```python
import functools

import jax
import jax.numpy as jnp
from jax import lax
from jax.experimental import pallas as pl
from jax.experimental.pallas import tpu as pltpu
from jax.sharding import PartitionSpec as P

ROUNDS = 2
MESH = pl.DeviceIdType.MESH
F32 = jnp.float32
BF16 = jnp.bfloat16
epsilon = 1e-06

GROUP = 16
CHIPS = 8
PIX = 512
FRM = 256
COMP = 256
ROWS = COMP // GROUP
HALO = 128
SPLIT = 1
PART = PIX // SPLIT
HALF = COMP // 2
TAPS = 257


def far_first(steps, hops):
    return sorted(steps, key=lambda step: -hops(*step))


Y_STEPS = (2, 1, 3, 0)
CHIP_STEPS = far_first(
    [(dx, dzh) for dx in range(4) for dzh in range(2) if dx or dzh],
    lambda dx, dzh: min(dx, 4 - dx) + 4 * dzh,
)
PIX_STEPS = far_first(
    [(dx, dzh, dc) for dx in range(4) for dzh in range(2) for dc in range(2) if dx or dzh or dc],
    lambda dx, dzh, dc: min(dx, 4 - dx) + 4 * dzh + 0.5 * dc,
)


def dot_nn(a, b):
    return lax.dot_general(a, b, (((1,), (0,)), ((), ())), preferred_element_type=F32)


def dot_nt(a, b):
    return lax.dot_general(a, b, (((1,), (1,)), ((), ())), preferred_element_type=F32)


def split(value):
    high = value.astype(BF16)
    return high, (value - high.astype(F32)).astype(BF16)


def product(gram, whole):
    both = dot_nn(jnp.concatenate(split(gram), axis=0), whole)
    return both[:ROWS] + both[ROWS:]


def diagonal_of(gram, block):
    row = lax.broadcasted_iota(jnp.int32, gram.shape, 0)
    column = lax.broadcasted_iota(jnp.int32, gram.shape, 1)
    return jnp.sum(jnp.where(column == row + block * ROWS, gram, 0.0), axis=1, keepdims=True)


def rows_of(index, count=ROWS):
    return pl.ds(pl.multiple_of(index * count, count), count)


def wait_bytes(ref, sem):
    pltpu.make_async_copy(ref, ref, sem).wait()


def summed(inbox, count):
    total = inbox[0].astype(F32)
    for slot in range(1, count):
        total = total + inbox[slot].astype(F32)
    return total


NUMER, GRAM, SHARE, LOW, CORE_GRAM, CORE, CHIP, NEAR, FAR, RELAY = 0, 2, 3, 5, 7, 8, 9, 10, 11, 12
ACROSS = 14
PHASES = 15


def kernel(
    movie_hbm, taps_hbm, scale_hbm, base_hbm, spatial_hbm, temporal_hbm,
    s_out, t_out,
    padded, taps_v, scale_v, base_v, spatial_v, temporal_v,
    coef, norm_t, s_zero_t, s_own, t_own, t_across, t_bf, t_turned,
    gram_part, gram_in, gram_own, numer_part, numer_in, s_bf, s_low,
    mixed_part, core_in, chip_part, chip_in,
    load_sem, halo_send, halo_recv, send_sem, recv_sem, met,
):
    p = lax.axis_index("pix")
    f = lax.axis_index("frm")
    x, zh, c = lax.div(p, 4), lax.rem(lax.div(p, 2), 2), lax.rem(p, 2)
    zl, y = lax.div(f, 4), lax.rem(f, 4)
    pix_block = zh * 4 + x
    t_block = c * CHIPS + pix_block

    def pix_at(dx, dzh, dc):
        return lax.rem(x + dx, 4), lax.rem(zh + dzh, 2), lax.rem(c + dc, 2)

    def pix_device(ox, ozh, oc):
        return ((ox * 2 + ozh) * 2 + oc, f)

    def frm_at(dzl, dy):
        return lax.rem(zl + dzl, 4) * 4 + lax.rem(y + dy, 4)

    mirrored, across, beside = 3 - zl, lax.rem(zl + 2, 4), zl + 1 - 2 * lax.rem(zl, 2)

    def in_plane(plane, steps=Y_STEPS):
        return [plane * 4 + lax.rem(y + dy, 4) for dy in steps]

    planes = (mirrored, across, beside, zl)
    frm_others = [
        plane * 4 + lax.rem(y + dy, 4) for dy in Y_STEPS for plane in (planes if dy else planes[:3])
    ]

    barrier = pltpu.get_barrier_semaphore()
    x_line = [pix_device(*pix_at(dx, 0, 0)) for dx in (2, 1, 3)]
    partner = pix_device(x, zh, 1 - c)
    z_two = [(pix_device(x, 1 - zh, c)[0], frm_at(2, 0)), (p, frm_at(2, 0))]
    z_line = [(p, plane * 4 + y) for plane in (mirrored, across, beside)]
    y_line = [(p, frm_at(0, dy)) for dy in (2, 1, 3)]

    def signal(sem, targets):
        for target in targets:
            pl.semaphore_signal(sem, inc=1, device_id=target, device_id_type=MESH)

    greeted = [*z_line, z_two[0], *x_line, *y_line, partner]
    signal(barrier, greeted)
    corner_right = jnp.logical_and(y == 3, f < GROUP - 1)
    corner_left = jnp.logical_and(y == 0, f > 0)

    @pl.when(corner_right)
    def _():
        signal(barrier, [(p, f + 1)])

    @pl.when(corner_left)
    def _():
        signal(barrier, [(p, f - 1)])

    loads = [
        pltpu.make_async_copy(src, dst, load_sem.at[i])
        for i, (src, dst) in enumerate(
            (
                (movie_hbm, padded.at[:, pl.ds(HALO, FRM)]),
                (temporal_hbm, temporal_v),
                (spatial_hbm, spatial_v),
                (taps_hbm, taps_v),
                (scale_hbm, scale_v),
                (base_hbm, base_v),
            )
        )
    ]
    for copy in loads:
        copy.start()

    def remote(src, dst, sem, target):
        return pltpu.make_async_remote_copy(
            src_ref=src,
            dst_ref=dst,
            send_sem=send_sem.at[sem],
            recv_sem=recv_sem.at[sem],
            device_id=target,
            device_id_type=MESH,
        )

    cornered = jnp.logical_or(corner_right, corner_left)

    @pl.when(cornered)
    def _():
        pl.semaphore_wait(barrier, len(greeted) + 1)

    @pl.when(jnp.logical_not(cornered))
    def _():
        pl.semaphore_wait(barrier, len(greeted))

    met_frm, met_two, met_line, met_pix = (met.at[i] for i in range(4))
    loads[0].wait()
    halos = []
    for h in range(SPLIT):
        pixels = pl.ds(h * PART, PART)
        for side, (source, target, step) in enumerate(
            ((FRM, 0, 1), (HALO, HALO + FRM, GROUP - 1))
        ):
            halos.append(
                pltpu.make_async_remote_copy(
                    src_ref=padded.at[pixels, pl.ds(source, HALO)],
                    dst_ref=padded.at[pixels, pl.ds(target, HALO)],
                    send_sem=halo_send.at[2 * h + side],
                    recv_sem=halo_recv.at[2 * h + side],
                    device_id=(p, lax.rem(f + step, GROUP)),
                    device_id_type=MESH,
                )
            )
    has_right, has_left = f < GROUP - 1, f > 0

    @pl.when(has_right)
    def _():
        for copy in halos[0::2]:
            copy.start()

    @pl.when(has_left)
    def _():
        for copy in halos[1::2]:
            copy.start()

    signal(met_frm, z_line)
    signal(met_two, [*z_two, *x_line, partner])

    def make_gram(r):
        t_now = t_bf[r]
        t_half = t_bf[r, rows_of(c, HALF), :]
        gram_part[r] = dot_nt(t_now, t_half).astype(BF16)

    def send_gram(r):
        for other in frm_others:
            remote(
                gram_part.at[r, rows_of(other)], gram_in.at[r, f], r * PHASES + GRAM, (p, other)
            ).start()
        gram_in[r, f] = gram_part[r, rows_of(f), :]

    def finish_gram(r):
        wait_bytes(gram_in.at[r, pl.ds(0, GROUP - 1)], recv_sem.at[r * PHASES + GRAM])
        half = pl.ds(pl.multiple_of(c * HALF, HALF), HALF)
        gram_own[r, :, half] = summed(gram_in.at[r], GROUP)
        mine = gram_own.at[r, :, half]
        copy = remote(mine, mine, r * PHASES + CORE_GRAM, pix_device(x, zh, 1 - c))
        copy.start()
        parts = [product(gram_own[r, :, half], s_bf[r, h, rows_of(c, HALF), :]) for h in range(SPLIT)]
        copy.wait_recv()
        rest = pl.ds(pl.multiple_of((1 - c) * HALF, HALF), HALF)
        diagonal = diagonal_of(gram_own[r], f)
        denoms = []
        for h in range(SPLIT):
            denom = parts[h] + product(gram_own[r, :, rest], s_bf[r, h, rows_of(1 - c, HALF), :])
            error = s_own[h] - s_bf[r, h, rows_of(f), :].astype(F32)
            denoms.append(denom + diagonal * error)
        return denoms

    loads[1].wait()
    t_bf[0] = temporal_v[...].astype(BF16)
    make_gram(0)
    pl.semaphore_wait(met_frm, len(z_line))
    send_gram(0)

    @pl.when(f == 0)
    def _():
        padded[:, pl.ds(0, HALO)] = jnp.zeros((PIX, HALO), BF16)

    @pl.when(f == GROUP - 1)
    def _():
        padded[:, pl.ds(HALO + FRM, HALO)] = jnp.zeros((PIX, HALO), BF16)

    for copy in loads[2:]:
        copy.wait()
    coef[...] = jnp.zeros_like(coef)
    centre = lax.broadcasted_iota(jnp.int32, (1, TAPS), 1) == HALO
    coef[:, pl.ds(0, TAPS)] = jnp.where(centre, 1.0, 0.0).astype(F32) - taps_v[...][None]
    band_t = pltpu.roll(
        jnp.broadcast_to(coef[...], (FRM, 2 * FRM)), 0, 1, stride=1, stride_axis=0
    ).astype(BF16)
    spatial_t = spatial_v[...].T
    for h in range(SPLIT):
        s_zero_t[h] = spatial_t[:, h * PART : (h + 1) * PART]
        s_bf[0, h] = s_zero_t[h].astype(BF16)
        s_own[h] = s_zero_t[h, rows_of(f), :]
    t_own[...] = temporal_v[rows_of(t_block), :]
    pl.semaphore_wait(met_two, len(z_two) + len(x_line) + 1)
    signal(met_line, [*x_line, partner])

    def send_numer(r, h, others):
        for other in others:
            remote(
                numer_part.at[r, h, rows_of(other)],
                numer_in.at[r, h, f],
                r * PHASES + NUMER + h,
                (p, other),
            ).start()

    for h in range(SPLIT):
        pixels = pl.ds(h * PART, PART)

        @pl.when(has_left)
        def _():
            halos[2 * h].wait_recv()

        @pl.when(has_right)
        def _():
            halos[2 * h + 1].wait_recv()

        mixed = dot_nt(band_t, padded[pixels, :])
        scaled = scale_v[pixels][None] * mixed + base_v[pixels][None]
        norm_t[h] = jnp.maximum(scaled, 0.0).astype(BF16)
        numer_part[0, h] = dot_nn(t_bf[0], norm_t[h]).astype(BF16)
        send_numer(0, h, frm_others)
        numer_in[0, h, f] = numer_part[0, h, rows_of(f), :]

    chips, ends = [], []
    for dx, dzh in CHIP_STEPS:
        ox, ozh, _ = pix_at(dx, dzh, 0)
        chips.append((ox, ozh, pix_device(ox, ozh, c)))
    for dx in (2, 1, 3, 0):
        for ozh in range(2):
            ox = lax.rem(x + dx, 4)
            ends.append((ox, ozh, ((ox * 2 + ozh) * 2 + c, frm_at(2, 0))))

    pl.semaphore_wait(met_line, len(x_line) + 1)
    signal(met_pix, [partner])

    def left(r, *names):
        last = r == ROUNDS - 1
        temporal_rows = t_out if last else t_bf.at[ROUNDS - 1]
        refs = {
            GRAM: gram_in.at[r, pl.ds(0, GROUP - 1)],
            CORE_GRAM: gram_own.at[r, :, pl.ds(0, HALF)],
            CORE: core_in.at[r],
            CHIP: chip_in.at[r, pl.ds(0, CHIPS if last else CHIPS - 1)],
            NEAR: temporal_rows.at[pl.ds(0, (4 if last else 7) * ROWS)],
            FAR: temporal_rows.at[pl.ds(0, (4 if last else 8) * ROWS)],
            LOW: s_low.at[0, pl.ds(0, 3)],
            LOW + 1: s_low.at[pl.ds(0, 3)],
            ACROSS: t_across,
            RELAY: t_out.at[pl.ds(0, 64)],
            RELAY + 1: t_out.at[pl.ds(0, 64)],
        }
        for h in range(SPLIT):
            refs[NUMER + h] = numer_in.at[r, h, pl.ds(0, GROUP - 1)]
            refs[SHARE + h] = s_bf.at[r + 1, h, pl.ds(0, COMP - ROWS)]
        for name in names:
            wait_bytes(refs[name], send_sem.at[r * PHASES + name])

    spatial_phases = [GRAM, CORE_GRAM, *(NUMER + h for h in range(SPLIT))]
    spatial_phases += [SHARE + h for h in range(SPLIT)]

    for r in range(ROUNDS):
        last = r == ROUNDS - 1
        at = r * PHASES
        denoms = finish_gram(r)
        for h in range(SPLIT):
            wait_bytes(numer_in.at[r, h, pl.ds(0, GROUP - 1)], recv_sem.at[at + NUMER + h])
            numer = summed(numer_in.at[r, h], GROUP)
            s_new = s_own[h] * numer / (denoms[h] + epsilon)
            s_own[h] = s_new
            high, low = split(s_new)
            s_bf[r + 1, h, rows_of(f), :] = high
            mine = s_bf.at[r + 1, h, rows_of(f)]
            for other in frm_others:
                remote(mine, mine, at + SHARE + h, (p, other)).start()
            if last:
                s_low[y, zl, :, pl.ds(h * PART, PART)] = low

        numer_t = second_t = 0.0
        for h in range(SPLIT):
            wait_bytes(s_bf.at[r + 1, h, pl.ds(0, COMP - ROWS)], recv_sem.at[at + SHARE + h])
            s_now = s_bf[r + 1, h]
            numer_t = numer_t + dot_nt(s_now, norm_t[h])
            if last:
                second = dot_nn(t_turned[...], s_now).astype(BF16)
            else:
                second = s_now
            second_t = second_t + dot_nt(s_now, second)
        mixed_part[r, :, pl.ds(0, FRM)] = numer_t.astype(BF16)
        mixed_part[r, :, pl.ds(FRM, COMP)] = second_t.astype(BF16)
        remote(
            mixed_part.at[r, rows_of(1 - c, HALF)],
            core_in.at[r],
            at + CORE,
            pix_device(x, zh, 1 - c),
        ).start()
        if last:
            for target in z_line:
                remote(s_low.at[y, zl], s_low.at[y, zl], at + LOW, target).start()
        wait_bytes(core_in.at[r], recv_sem.at[at + CORE])
        chip_sum = mixed_part[r, rows_of(c, HALF), :].astype(F32) + core_in[r].astype(F32)
        chip_part[r] = chip_sum.astype(BF16)
        if not r:
            pl.semaphore_wait(met_pix, 1)
        for ox, ozh, target in ends if last else chips:
            remote(
                chip_part.at[r, rows_of(ozh * 4 + ox)],
                chip_in.at[r, pix_block],
                at + CHIP,
                target,
            ).start()
        if last:
            wait_bytes(s_low.at[0, pl.ds(0, 3)], recv_sem.at[at + LOW])
            for target in y_line:
                remote(s_low.at[y], s_low.at[y], at + LOW + 1, target).start()
        if not r:

            @pl.when(has_right)
            def _():
                for copy in halos[0::2]:
                    copy.wait_send()

            @pl.when(has_left)
            def _():
                for copy in halos[1::2]:
                    copy.wait_send()

        left(r, *spatial_phases, CORE)
        if not last:
            chip_in[r, pix_block] = chip_part[r, rows_of(pix_block), :]
            wait_bytes(chip_in.at[r, pl.ds(0, CHIPS - 1)], recv_sem.at[at + CHIP])
            total = summed(chip_in.at[r], CHIPS)
            gram_t = total[:, FRM:]
            error = t_own[...] - t_bf[r, rows_of(t_block), :].astype(F32)
            denom_t = product(gram_t, t_bf[r]) + diagonal_of(gram_t, t_block) * error
            t_new = t_own[...] * total[:, :FRM] / (denom_t + epsilon)
            t_own[...] = t_new
            t_bf[r + 1, rows_of(t_block), :] = t_new.astype(BF16)
            mine = t_bf.at[r + 1, rows_of(t_block)]
            for dx, dzh, dc in PIX_STEPS:
                sem = at + (FAR if dzh else NEAR)
                remote(mine, mine, sem, pix_device(*pix_at(dx, dzh, dc))).start()
            remote(t_own, t_across, at + ACROSS, (p, frm_at(2, 0))).start()
            for part, sem, count in ((0, NEAR, CHIPS - 1), (1, FAR, CHIPS)):
                wait_bytes(t_bf.at[r + 1, pl.ds(0, count * ROWS)], recv_sem.at[at + sem])
                if part:
                    make_gram(r + 1)
                    send_gram(r + 1)
                group = lax.rem(zh + part, 2)
                spans = [pl.ds(pl.multiple_of(b * HALF + group * 64, 64), 64) for b in range(2)]
                t_rows = jnp.concatenate([t_bf[r + 1, span, :] for span in spans], axis=0)
                odd = lax.rem(zl + group, 2)
                far_plane = across + odd * (mirrored - across)
                near_plane = zl + odd * (beside - zl)
                for h in range(SPLIT):
                    rows = dot_nn(t_rows, norm_t[h]).astype(BF16)
                    for b, span in enumerate(spans):
                        numer_part[r + 1, h, span, :] = rows[b * 64 : (b + 1) * 64]
                for h in range(SPLIT):
                    send_numer(r + 1, h, in_plane(far_plane) + in_plane(near_plane, Y_STEPS[:3]))

                    @pl.when(odd > 0)
                    def _():
                        send_numer(r + 1, h, in_plane(near_plane, Y_STEPS[3:]))

            for h in range(SPLIT):
                numer_in[r + 1, h, f] = numer_part[r + 1, h, rows_of(f), :]
            t_turned[...] = t_bf[r + 1].T
        else:
            wait_bytes(t_across, recv_sem.at[at - PHASES + ACROSS])
            wait_bytes(chip_in.at[r], recv_sem.at[at + CHIP])
            total = summed(chip_in.at[r], CHIPS)
            t_across[...] = t_across[...] * total[:, :FRM] / (total[:, FRM:] + epsilon)
            for _, ozh, target in ends:
                place = t_out.at[rows_of(t_block)]

                @pl.when(ozh == zh)
                def _():
                    remote(t_across, place, at + NEAR, target).start()

                @pl.when(ozh != zh)
                def _():
                    remote(t_across, place, at + FAR, target).start()

            for part, sem, count in ((0, NEAR, 4), (1, FAR, 4)):
                wait_bytes(t_out.at[pl.ds(0, count * ROWS)], recv_sem.at[at + sem])
                group = lax.rem(zh + part, 2)
                got = t_out.at[pl.ds(pl.multiple_of(c * HALF + group * 64, 64), 64)]
                remote(got, got, at + RELAY + part, pix_device(x, zh, 1 - c)).start()
            left(r - 1, CHIP, NEAR, FAR, ACROSS)
            left(r, CHIP, LOW, LOW + 1)
            wait_bytes(s_low.at[pl.ds(0, 3)], recv_sem.at[at + LOW + 1])
            for h in range(SPLIT):
                pixels = pl.ds(h * PART, PART)
                low = jnp.concatenate(
                    [s_low[block % 4, block // 4, :, pixels] for block in range(GROUP)], axis=0
                )
                s_out[pixels, :] = (s_bf[r + 1, h].astype(F32) + low.astype(F32)).T
            for part in range(2):
                wait_bytes(t_out.at[pl.ds(0, 64)], recv_sem.at[at + RELAY + part])
            left(r, NEAR, FAR, RELAY, RELAY + 1)


def hand_on(s_v, t_v, s_out, t_out, sem):
    copies = [
        pltpu.make_async_copy(s_v, s_out, sem.at[0]),
        pltpu.make_async_copy(t_v, t_out, sem.at[1]),
    ]
    for copy in copies:
        copy.start()
    for copy in copies:
        copy.wait()


def on_device(movie, taps, scale, base, spatial, temporal):
    hbm = pl.BlockSpec(memory_space=pltpu.HBM)
    vmem = pl.BlockSpec(memory_space=pltpu.VMEM)
    shapes = (
        jax.ShapeDtypeStruct((PIX, COMP), F32),
        jax.ShapeDtypeStruct((COMP, FRM), F32),
    )
    operands = [
        pltpu.with_memory_space_constraint(array, pltpu.HBM)
        for array in (movie, taps, scale, base, spatial, temporal)
    ]
    s, t = pl.pallas_call(
        kernel,
        out_shape=shapes,
        in_specs=[hbm] * 6,
        out_specs=(vmem, vmem),
        scratch_shapes=[
            pltpu.VMEM((PIX, 2 * FRM), BF16),
            pltpu.VMEM((TAPS,), F32),
            pltpu.VMEM((PIX,), F32),
            pltpu.VMEM((PIX,), F32),
            pltpu.VMEM((PIX, COMP), F32),
            pltpu.VMEM((COMP, FRM), F32),
            pltpu.VMEM((1, 2 * FRM), F32),
            pltpu.VMEM((SPLIT, FRM, PART), BF16),
            pltpu.VMEM((SPLIT, COMP, PART), F32),
            pltpu.VMEM((SPLIT, ROWS, PART), F32),
            pltpu.VMEM((ROWS, FRM), F32),
            pltpu.VMEM((ROWS, FRM), F32),
            pltpu.VMEM((ROUNDS, COMP, FRM), BF16),
            pltpu.VMEM((FRM, COMP), BF16),
            pltpu.VMEM((ROUNDS, COMP, HALF), BF16),
            pltpu.VMEM((ROUNDS, GROUP, ROWS, HALF), BF16),
            pltpu.VMEM((ROUNDS, ROWS, COMP), F32),
            pltpu.VMEM((ROUNDS, SPLIT, COMP, PART), BF16),
            pltpu.VMEM((ROUNDS, SPLIT, GROUP, ROWS, PART), BF16),
            pltpu.VMEM((ROUNDS + 1, SPLIT, COMP, PART), BF16),
            pltpu.VMEM((4, 4, ROWS, PIX), BF16),
            pltpu.VMEM((ROUNDS, COMP, FRM + COMP), BF16),
            pltpu.VMEM((ROUNDS, HALF, FRM + COMP), BF16),
            pltpu.VMEM((ROUNDS, HALF, FRM + COMP), BF16),
            pltpu.VMEM((ROUNDS, CHIPS, ROWS, FRM + COMP), BF16),
            pltpu.SemaphoreType.DMA((6,)),
            pltpu.SemaphoreType.DMA((2 * SPLIT,)),
            pltpu.SemaphoreType.DMA((2 * SPLIT,)),
            pltpu.SemaphoreType.DMA((ROUNDS * PHASES,)),
            pltpu.SemaphoreType.DMA((ROUNDS * PHASES,)),
            pltpu.SemaphoreType.REGULAR((4,)),
        ],
        compiler_params=pltpu.CompilerParams(
            collective_id=0, has_side_effects=True, vmem_limit_bytes=40 << 20
        ),
    )(*operands)
    return pl.pallas_call(
        hand_on,
        out_shape=shapes,
        in_specs=[vmem, vmem],
        out_specs=(hbm, hbm),
        scratch_shapes=[pltpu.SemaphoreType.DMA((2,))],
        compiler_params=pltpu.CompilerParams(vmem_limit_bytes=40 << 20),
    )(s, t)


def solution(mesh):
    placed = (P("pix", "frm"), P(), P("pix"), P("pix"), P("pix", None), P(None, "frm"))
    return jax.shard_map(
        on_device,
        mesh=mesh,
        in_specs=placed,
        out_specs=(P("pix", None), P(None, "frm")),
        check_vma=False,
    )
```
